32 devices in a mesh: energy: 8 (over z, x), tile: 4 (over y, core).
Axes of the slice: x: 2, y: 2, z: 4, core: 2. Of those that a mesh axis runs over, the one named last changes fastest.
Arguments:
- object_tiles: float32 [8, 2, 4, 512, 512], P('energy', None, 'tile'), may hold values from -6 to 6
- probe_wave: float32 [8, 2, 256, 256], P('energy'), may hold values from -6 to 6
- measured: bfloat16 [8, 4, 16, 256, 256], P('energy', 'tile'), may hold values from 0 to 2
- positions: int32 [4, 16, 2], P('tile'), may hold values from 0 to 511, as said below
- materials: float32 [2, 8, 8], replicated, may hold values from -6 to 6
Outputs:
- fitted: float32 [8, 2, 4, 512, 512], P('energy', None, 'tile')
The draws below stay inside these ranges and needn't reach their ends.
Inputs may be any that keep to these rules, and one draw needn't show every extreme that they name: `positions`: each entry is the corner of a 256 x 256 patch, given inside its tile; in every tile some patch has row corner 512 - 1 and some has column corner 512 - 1.
All inputs are finite; a program needn't handle non-finite values.
Results may differ from the reference program's by a relative error of at most 0.0013.
Values sent between devices are 32-bit elements; how exact they have to be, the bound alone decides.
A program may use at most 64 MiB of HBM per device.

```python
import math
import jax
import jax.numpy as jnp
from jax import lax

PATCH = 256
TILE_PX = 512
TILE_COLS = 4
PATCHES = 16
MATERIALS = 8
FIT_STEPS = 10
ENERGIES = 8
TILES = 4


def draw_positions(key, part):
    base = jax.random.fold_in(key, 11)
    row_key, col_key = jax.random.split(base)
    row_draw = jax.random.randint(row_key, (TILES, PATCHES), 0, TILE_PX, dtype=jnp.int32)
    col_draw = jax.random.randint(col_key, (TILES, PATCHES), 0, TILE_PX, dtype=jnp.int32)
    col_draw = col_draw.at[:, 0].set(TILE_PX - 1)
    row_draw = row_draw.at[:, 1].set(TILE_PX - 1)
    col_draw = col_draw.at[:, 1].set(TILE_PX - 1)
    corners = jnp.stack([row_draw, col_draw], -1).astype(jnp.int32)
    return corners


def steps_of(key, shape, cuts, smallest, top_value):
    def one(position, blocks):
        steps = jax.random.uniform(jax.random.fold_in(jax.random.fold_in(key, 6), position), (blocks,), jnp.float32, smallest / len(cuts), top_value / len(cuts))
        return jnp.repeat(jnp.exp(steps), shape[position] // blocks).reshape((-1,) + (1,) * (len(shape) - position - 1))

    gain = one(*cuts[0])
    for cut in cuts[1:]:
        gain = gain * one(*cut)
    return gain


def normal_values(stream_key, extent, width, limit, pieces=(), kind=jnp.bfloat16):
    level = steps_of(stream_key, extent, pieces, -0.22, 0.18) if pieces else 1.0
    entries = jax.random.normal(stream_key, extent, jnp.float32) * width * level
    return jnp.minimum(jnp.maximum(entries, -limit), limit).astype(kind)


def setup_inputs(seed: int = 0) -> dict:
    key_list = jax.random.split(jax.random.key(seed), 6)
    object_tiles = normal_values(key_list[0], (ENERGIES, 2, TILES, TILE_PX, TILE_PX), 1.0, 6.0, ((0, 8), (2, 4)), jnp.float32)
    probe_wave = normal_values(key_list[1], (ENERGIES, 2, PATCH, PATCH), 1.0, 6.0, ((0, 8),), jnp.float32)
    measured = jnp.clip(2.0 * jax.random.uniform(key_list[2], (ENERGIES, TILES, PATCHES, PATCH, PATCH), jnp.float32) ** steps_of(key_list[2], (ENERGIES, TILES, PATCHES, PATCH, PATCH), ((0, 8), (1, 4)), -0.2, 0.2), 0.0, 2.0).astype(jnp.bfloat16)
    positions = draw_positions(jax.random.fold_in(key_list[5], 71), 0)
    materials = normal_values(key_list[4], (2, ENERGIES, MATERIALS), 1.0, 6.0, (), jnp.float32)
    return {"object_tiles": object_tiles, "probe_wave": probe_wave, "measured": measured, "positions": positions, "materials": materials}


amplitude_floor = 0.5

def fourier_tables(length, direction):
    counter = jnp.arange(length, dtype=jnp.int32)
    products = counter[:, None] * counter[None, :] % length
    angles = 2.0 * math.pi / length * products.astype(jnp.float32)
    cosine = jnp.cos(angles)
    sine = direction * jnp.sin(angles)
    left_table = jnp.concatenate([jnp.concatenate([cosine, sine], 1), jnp.concatenate([-sine, cosine], 1)], 0).astype(jnp.bfloat16)
    right_table = jnp.concatenate([jnp.concatenate([cosine, -sine], 1), jnp.concatenate([sine, cosine], 1)], 0).astype(jnp.bfloat16)
    return (left_table, right_table)

def transform(real_part, imag_part, left_table, right_table):
    length = real_part.shape[0]
    stacked = jnp.concatenate([real_part, imag_part], 0).astype(jnp.bfloat16)
    inner = jnp.dot(left_table, stacked, preferred_element_type=jnp.float32)
    beside = jnp.concatenate([inner[:length], inner[length:]], 1).astype(jnp.bfloat16)
    outer = jnp.dot(beside, right_table, preferred_element_type=jnp.float32) / length
    return (outer[:, :length], outer[:, length:])

def patch_gradient(field_real, field_imag, probe_real, probe_imag, amplitude, row_start, col_start, tables):
    length = probe_real.shape[0]
    piece_real = lax.dynamic_slice(field_real, (row_start, col_start), (length, length))
    piece_imag = lax.dynamic_slice(field_imag, (row_start, col_start), (length, length))
    exit_real = probe_real * piece_real - probe_imag * piece_imag
    exit_imag = probe_real * piece_imag + probe_imag * piece_real
    far_real, far_imag = transform(exit_real, exit_imag, tables[0], tables[1])
    magnitude = jnp.sqrt(far_real * far_real + far_imag * far_imag)
    factor = amplitude.astype(jnp.float32) / jnp.maximum(magnitude, amplitude_floor) - 1.0
    back_real, back_imag = transform(factor * far_real, factor * far_imag, tables[2], tables[3])
    return (probe_real * back_real + probe_imag * back_imag, probe_real * back_imag - probe_imag * back_real)

def fit_materials(data, materials):
    high = lax.Precision.HIGHEST
    gram = jnp.einsum('rem,ren->mn', materials, materials, precision=high)
    rate = 1.0 / jnp.trace(gram)
    target = jnp.einsum('rem,rep->mp', materials, data, precision=high)

    def descend(number, coefficients):
        slope = jnp.dot(gram, coefficients, precision=high) - target
        return jnp.maximum(coefficients - rate * slope, 0.0)
    return lax.fori_loop(0, FIT_STEPS, descend, jnp.zeros_like(target))

def energy_update(object_one, probe_one, measured_one, positions):
    right_strip = jnp.roll(object_one, -1, axis=1)[:, :, :, :PATCH]
    widened = jnp.concatenate([object_one, right_strip], 3)
    lower_strip = jnp.roll(widened, -TILE_COLS, axis=1)[:, :, :PATCH, :]
    extended = jnp.concatenate([widened, lower_strip], 2)
    forward = fourier_tables(PATCH, 1.0)
    inverse = fourier_tables(PATCH, -1.0)
    tables = (forward[0], forward[1], inverse[0], inverse[1])
    flat_measured = measured_one.reshape(TILES * PATCHES, PATCH, PATCH)
    flat_corners = positions.reshape(TILES * PATCHES, 2)
    anchor = jnp.zeros((), jnp.int32)

    def accumulate(number, gradient):
        tile_index = (number // PATCHES).astype(jnp.int32)
        row_start = flat_corners[number, 0].astype(jnp.int32)
        col_start = flat_corners[number, 1].astype(jnp.int32)
        field = lax.dynamic_index_in_dim(extended, tile_index, 1, False)
        term_real, term_imag = patch_gradient(field[0], field[1], probe_one[0], probe_one[1], flat_measured[number], row_start, col_start, tables)
        current = lax.dynamic_slice(gradient, (anchor, tile_index, row_start, col_start), (2, 1, PATCH, PATCH))
        added = current + jnp.stack([term_real, term_imag])[:, None]
        return lax.dynamic_update_slice(gradient, added, (anchor, tile_index, row_start, col_start))
    gradient = lax.fori_loop(0, TILES * PATCHES, accumulate, jnp.zeros_like(extended))
    from_above = jnp.roll(gradient[:, :, TILE_PX:, :], TILE_COLS, axis=1)
    upper = jnp.concatenate([gradient[:, :, :PATCH, :] + from_above, gradient[:, :, PATCH:TILE_PX, :]], 2)
    from_left = jnp.roll(upper[:, :, :, TILE_PX:], 1, axis=1)
    summed = jnp.concatenate([upper[:, :, :, :PATCH] + from_left, upper[:, :, :, PATCH:TILE_PX]], 3)
    peak = jnp.max(probe_one[0] * probe_one[0] + probe_one[1] * probe_one[1])
    return object_one + summed / peak

def reference(object_tiles, probe_wave, measured, positions, materials):
    updated = lax.map(lambda inputs: energy_update(inputs[0], inputs[1], inputs[2], positions), (object_tiles, probe_wave, measured))
    data = updated.transpose(1, 0, 2, 3, 4).reshape(2, ENERGIES, TILES * TILE_PX * TILE_PX)
    coefficients = fit_materials(data, materials)
    spectra = jnp.einsum('rem,mp->rep', materials, coefficients, precision=lax.Precision.HIGHEST)
    spectra = spectra.reshape(2, ENERGIES, TILES, TILE_PX, TILE_PX).transpose(1, 0, 2, 3, 4)
    return spectra
```

```python
import functools
import math

import jax
import jax.numpy as jnp
import numpy as np
from jax import lax
from jax.experimental import pallas as pl
from jax.experimental.pallas import tpu as pltpu
from jax.sharding import PartitionSpec as P

TILE_COLS = 4
FIT_STEPS = 10
LANES = 128
VMEM_LIMIT = 24 * 1024 * 1024


amplitude_floor = 0.5


def shifted(value, axis, steps):
    count = lax.axis_size(axis)
    pairs = [(source, (source + steps) % count) for source in range(count)]
    return lax.ppermute(value, axis, pairs)


def trig_parts(rows, columns, length):
    angles = 2.0 * math.pi / length * (rows[:, None] * columns[None, :] % length)
    return np.stack([np.cos(angles), np.sin(angles)]).astype(np.float32).astype(jnp.bfloat16)


def fourier_parts(length):
    counter = np.arange(length, dtype=np.int64)
    half = counter[: length // 2]
    left = np.stack([trig_parts(half, counter[parity::2], length) for parity in range(2)])
    return jnp.asarray(left), jnp.asarray(trig_parts(counter, counter, length))


def joined(top_left, top_right, bottom_left, bottom_right):
    return jnp.concatenate(
        [
            jnp.concatenate([top_left, top_right], 1),
            jnp.concatenate([bottom_left, bottom_right], 1),
        ],
        0,
    )


def transform(even, odd, left_ref, right_ref):
    length = even.shape[0]
    half = length // 2
    one = jnp.dot(left_ref[0], even, preferred_element_type=jnp.float32)
    two = jnp.dot(left_ref[1], odd, preferred_element_type=jnp.float32)
    upper = (one + two).astype(jnp.bfloat16)
    lower = (one - two).astype(jnp.bfloat16)
    beside = joined(upper[:half], upper[half:], lower[:half], lower[half:])
    outer = jnp.dot(beside, right_ref[...], preferred_element_type=jnp.float32)
    return outer[:, :length], outer[:, length:]


def window(ref, part, rows, block, shift, length):
    lane = lax.broadcasted_iota(jnp.int32, (rows.size, LANES), 1)
    back = lax.rem(LANES - shift, LANES)
    tiles = [
        pltpu.roll(ref[part, block + at, rows, :], back, 1) for at in range(length // LANES + 1)
    ]
    keep = lane < LANES - shift
    return jnp.concatenate(
        [jnp.where(keep, one, other) for one, other in zip(tiles[:-1], tiles[1:])], 1
    )


def add_window(ref, part, row, block, shift, term):
    length = term.shape[0]
    lane = lax.broadcasted_iota(jnp.int32, (length, LANES), 1)
    tiles = [pltpu.roll(term[:, at : at + LANES], shift, 1) for at in range(0, length, LANES)]
    keep = lane >= shift
    zero = jnp.zeros_like(tiles[0])
    for at, (one, other) in enumerate(zip(tiles + [zero], [zero] + tiles)):
        place = (part, block + at, pl.ds(row, length), slice(None))
        ref[place] = ref[place] + jnp.where(keep, one, other)


def patch_kernel(fold, phase, phases, *refs):
    first = phase == 0
    last = phase == phases - 1
    if first:
        corners_ref, object_ref, measured_ref, probe_ref, left_ref, right_ref = refs[:6]
        gradient, field, wave, change, terms, held, left, right, probe, split = refs[6:16]
        parts_left, parts_right, order, sems = refs[16:]
    else:
        lower_count = 1 if last and not fold else 0
        corners_ref, strip_ref = refs[:2]
        lower_ref = refs[2] if lower_count else None
        held, left, right, probe, split = refs[2 + lower_count : 7 + lower_count]
        refs = refs[12 + lower_count :]
        gradient, field, wave, change, terms = refs[:5]
        if last:
            main_out, side_out, below_out = refs[5:8]
        order, sems = refs[-2:]
    length = wave.shape[-1]
    half = length // 2
    pieces = length // LANES
    width = field.shape[1]
    blocks = width - pieces
    tile_px = blocks * LANES
    count = held.shape[0]
    limit = tile_px - length
    top = pl.ds(0, tile_px)
    bottom = pl.ds(tile_px, length)
    moves = []
    if first:
        moves.append((left_ref, parts_left))
        moves.append((right_ref, parts_right))
        for block in range(blocks):
            columns = pl.ds(block * LANES, LANES)
            moves.append((object_ref.at[:, :, columns], field.at[:, block, top, :]))
            if fold:
                source = object_ref.at[:, pl.ds(0, length), columns]
                moves.append((source, field.at[:, block, bottom, :]))
        for piece in range(pieces):
            columns = pl.ds(piece * LANES, LANES)
            moves.append((probe_ref.at[:, :, columns], probe.at[:, piece]))
        moves.append((measured_ref, held))
    else:
        block = blocks + phase - 1
        moves.append((strip_ref, field.at[:, block, top, :]))
        if fold:
            moves.append((strip_ref.at[:, pl.ds(0, length), :], field.at[:, block, bottom, :]))
        elif last:
            for block in range(width):
                columns = pl.ds(block * LANES, LANES)
                moves.append((lower_ref.at[:, :, columns], field.at[:, block, bottom, :]))
    copies = [
        pltpu.make_async_copy(source, target, sems.at[number])
        for number, (source, target) in enumerate(moves)
    ]
    for copy in copies:
        copy.start()

    def rank(number):
        beyond = corners_ref[number, 1] - limit
        kind = sum((beyond > step * LANES).astype(jnp.int32) for step in range(phases - 1))
        if not fold:
            kind = jnp.where(corners_ref[number, 0] > limit, phases - 1, kind)
        return kind

    kinds = [rank(number) for number in range(count)]
    ends = [
        sum((kind <= step).astype(jnp.int32) for kind in kinds) for step in range(phases)
    ]
    place = [jnp.int32(0)] + ends[:-1]
    for number, kind in enumerate(kinds):
        spot = place[-1]
        for step in range(phases - 1):
            spot = jnp.where(kind == step, place[step], spot)
        order[spot] = number
        place = [
            value + (kind == step).astype(jnp.int32) for step, value in enumerate(place)
        ]
    begin = jnp.maximum(ends[phase - 1] - 2, 0) if phase else 0
    end = count - 1 if last else jnp.maximum(ends[phase] - 2, 0)

    if first:
        gradient[...] = jnp.zeros_like(gradient)
        terms[...] = jnp.zeros_like(terms)
        for copy in copies[:2]:
            copy.wait()
        for parity in range(2):
            cosine = parts_left[parity, 0]
            sine = parts_left[parity, 1]
            left[0, parity] = joined(cosine, sine, -sine, cosine)
            left[1, parity] = joined(cosine, -sine, sine, cosine)
        scale = jnp.asarray(1.0 / length, jnp.bfloat16)
        cosine = parts_right[0] * scale
        sine = parts_right[1] * scale
        right[0] = joined(cosine, -sine, sine, cosine)
        right[1] = joined(cosine, sine, -sine, cosine)
        copies = copies[2:]
    for copy in copies:
        copy.wait()
    if first:
        for parity in range(2):
            for part in range(2):
                for piece in range(pieces):
                    columns = slice(piece * LANES, (piece + 1) * LANES)
                    rows = pl.ds(parity, half, stride=2)
                    split[parity, part, :, columns] = probe[part, piece, rows, :]

    def corner(turn):
        number = order[turn]
        row = corners_ref[number, 0]
        col = corners_ref[number, 1]
        block = col // LANES
        return number, row, block, col - block * LANES

    def gather(turn):
        _, row, block, shift = corner(turn)
        for parity in range(2):
            rows = pl.ds(row + parity, half, stride=2)
            piece_real = window(field, 0, rows, block, shift, length)
            piece_imag = window(field, 1, rows, block, shift, length)
            probe_real = split[parity, 0]
            probe_imag = split[parity, 1]
            exit_real = probe_real * piece_real - probe_imag * piece_imag
            exit_imag = probe_real * piece_imag + probe_imag * piece_real
            wave[parity, :half, :] = exit_real.astype(jnp.bfloat16)
            wave[parity, half:, :] = exit_imag.astype(jnp.bfloat16)

    def scatter(turn):
        _, row, block, shift = corner(turn)
        add_window(gradient, 0, row, block, shift, terms[0])
        add_window(gradient, 1, row, block, shift, terms[1])

    def outward(turn):
        far_real, far_imag = transform(wave[0], wave[1], left.at[0], right.at[0])
        square = far_real * far_real + far_imag * far_imag
        scale = lax.rsqrt(jnp.maximum(square, amplitude_floor * amplitude_floor))
        factor = held[order[turn]].astype(jnp.float32) * scale - 1.0
        return factor * far_real, factor * far_imag

    def keep(parts):
        for part in range(2):
            for piece in range(pieces):
                change[part, piece] = parts[part][:, piece * LANES : (piece + 1) * LANES]

    def changed(parity):
        rows = pl.ds(parity, half, stride=2)
        return jnp.concatenate(
            [
                jnp.concatenate([change[part, piece, rows, :] for piece in range(pieces)], 1)
                for part in range(2)
            ],
            0,
        ).astype(jnp.bfloat16)

    def homeward():
        back_real, back_imag = transform(changed(0), changed(1), left.at[1], right.at[1])
        probe_real = jnp.concatenate([probe[0, piece] for piece in range(pieces)], 1)
        probe_imag = jnp.concatenate([probe[1, piece] for piece in range(pieces)], 1)
        return (
            probe_real * back_real + probe_imag * back_imag,
            probe_real * back_imag - probe_imag * back_real,
        )

    def step(turn, carry):
        scatter(jnp.maximum(turn - 1, 0))
        parts = outward(turn + 1)
        back = homeward()
        keep(parts)
        gather(jnp.minimum(turn + 2, count - 1))
        terms[0] = back[0]
        terms[1] = back[1]
        return carry

    ready = ends[phase] >= 2
    if not first:
        ready = jnp.logical_and(ready, ends[phase - 1] < 2)

    @pl.when(ready)
    def _():
        gather(0)
        keep(outward(0))
        gather(1)

    lax.fori_loop(begin, end, step, 0)
    if not last:
        return
    scatter(count - 2)
    back = homeward()
    terms[0] = back[0]
    terms[1] = back[1]
    scatter(count - 1)

    peak = jnp.max(probe[0] * probe[0] + probe[1] * probe[1])
    inverse = 1.0 / jnp.full((8, LANES), peak, jnp.float32)
    tall = 64
    inverse = jnp.concatenate([inverse] * (tall // 8), 0)

    def finish(wrapped, number, carry):
        place = (pl.ds(pl.multiple_of(number * tall, tall), tall), slice(None))
        beyond = pl.ds(pl.multiple_of(tile_px + number * tall, tall), tall)
        for part in range(2):
            for block in range(width):
                value = gradient[(part, block) + place]
                if wrapped:
                    value = value + gradient[part, block, beyond, :]
                share = value * inverse
                if block < blocks:
                    columns = slice(block * LANES, (block + 1) * LANES)
                    main_out[part, place[0], columns] = field[(part, block) + place] + share
                else:
                    columns = slice((block - blocks) * LANES, (block - blocks + 1) * LANES)
                    side_out[part, place[0], columns] = share
        return carry

    lax.fori_loop(0, length // tall, functools.partial(finish, fold), 0)
    lax.fori_loop(length // tall, tile_px // tall, functools.partial(finish, False), 0)
    if fold:
        below_out[...] = jnp.zeros_like(below_out)
    else:
        for block in range(width):
            columns = slice(block * LANES, (block + 1) * LANES)
            below_out[:, :, columns] = gradient[:, block, tile_px:, :] * inverse[:1]


def patch_calls(own_object, probe, measured, corners, fold, strips, lower):
    tile_px = own_object.shape[-1]
    length = probe.shape[-1]
    count = measured.shape[0]
    width = tile_px + length
    pieces = length // LANES
    phases = 1 + len(strips)
    vmem = pl.BlockSpec(memory_space=pltpu.VMEM)
    anywhere = pl.BlockSpec(memory_space=pl.ANY)
    smem = pl.BlockSpec(memory_space=pltpu.SMEM)
    single = jnp.float32
    brief = jnp.bfloat16
    sums = (2, width // LANES, width, LANES)
    moving = [
        jax.ShapeDtypeStruct(sums, single),
        jax.ShapeDtypeStruct(sums, single),
        jax.ShapeDtypeStruct((2, length, length), brief),
        jax.ShapeDtypeStruct((2, pieces, length, LANES), single),
        jax.ShapeDtypeStruct((2, length, length), single),
    ]
    fixed = [
        jax.ShapeDtypeStruct(measured.shape, brief),
        jax.ShapeDtypeStruct((2, 2, length, length), brief),
        jax.ShapeDtypeStruct((2, 2 * length, 2 * length), brief),
        jax.ShapeDtypeStruct((2, pieces, length, LANES), single),
        jax.ShapeDtypeStruct((2, 2, length // 2, length), single),
    ]
    below = (2, 8, LANES) if fold else (2, length, width)
    results = [
        jax.ShapeDtypeStruct(shape, single)
        for shape in [(2, tile_px, tile_px), (2, tile_px, length), below]
    ]
    parts_left, parts_right = fourier_parts(length)
    shared = [
        pltpu.SMEM((count,), jnp.int32),
        pltpu.SemaphoreType.DMA((3 + 3 * (width // LANES),)),
    ]
    params = pltpu.CompilerParams(vmem_limit_bytes=VMEM_LIMIT)
    cost = pl.CostEstimate(
        flops=8 * count * length**3, bytes_accessed=8 * tile_px * tile_px, transcendentals=0
    )
    state = pl.pallas_call(
        functools.partial(patch_kernel, fold, 0, phases),
        out_shape=moving + fixed,
        in_specs=[smem] + [anywhere] * 5,
        out_specs=[vmem] * len(moving + fixed),
        scratch_shapes=[
            pltpu.VMEM(parts_left.shape, brief),
            pltpu.VMEM(parts_right.shape, brief),
        ]
        + shared,
        compiler_params=params,
        cost_estimate=cost,
        name="patches_0",
    )(corners, own_object, measured, probe, parts_left, parts_right)
    held = state[len(moving) :]
    state = state[: len(moving)]
    for phase, strip in enumerate(strips, 1):
        last = phase == phases - 1
        more = [lower] if last and not fold else []
        lead = 2 + len(more) + len(held)
        out = pl.pallas_call(
            functools.partial(patch_kernel, fold, phase, phases),
            out_shape=moving + (results if last else []),
            in_specs=[smem] + [anywhere] * (1 + len(more)) + [vmem] * len(held + state),
            out_specs=[vmem] * (len(moving) + (len(results) if last else 0)),
            scratch_shapes=shared,
            input_output_aliases={lead + at: at for at in range(len(moving))},
            compiler_params=params,
            cost_estimate=cost,
            name=f"patches_{phase}",
        )(corners, strip, *more, *held, *state)
        state = out[: len(moving)]
    return out[len(moving) :]


def fit_scalars(materials_ref, energies, kinds):
    spectra = [
        [materials_ref[(part * energies + energy) * kinds + kind] for kind in range(kinds)]
        for part in range(2)
        for energy in range(energies)
    ]
    gram = [[None] * kinds for _ in range(kinds)]
    for one in range(kinds):
        for other in range(one, kinds):
            total = spectra[0][one] * spectra[0][other]
            for row in spectra[1:]:
                total = total + row[one] * row[other]
            gram[one][other] = total
            gram[other][one] = total
    trace = gram[0][0]
    for one in range(1, kinds):
        trace = trace + gram[one][one]
    return gram, trace


def fit_columns(materials_ref, step_ref, data, spectra, energies, kinds, rate, begin, wide):
    rows = data.shape[2]
    tall = 16 if rows % 16 == 0 else 8
    pairs = [(part, energy) for part in range(2) for energy in range(energies)]

    def chunk(number, carry):
        row = pl.multiple_of(number * tall, tall)
        place = (pl.ds(row, tall), pl.ds(begin, wide))
        target = [None] * kinds
        for part, energy in pairs:
            plane = data[(part, energy) + place]
            for kind in range(kinds):
                term = materials_ref[(part * energies + energy) * kinds + kind] * plane
                target[kind] = term if target[kind] is None else target[kind] + term
        target = [rate * value for value in target]
        current = [jnp.maximum(value, 0.0) for value in target]

        def descend(turn, current):
            following = []
            for one in range(kinds):
                total = target[one]
                for other in range(kinds):
                    total = total + step_ref[one * kinds + other] * current[other]
                following.append(jnp.maximum(total, 0.0))
            return following

        current = lax.fori_loop(1, FIT_STEPS, descend, current)
        for part, energy in pairs:
            total = None
            for kind in range(kinds):
                term = materials_ref[(part * energies + energy) * kinds + kind] * current[kind]
                total = term if total is None else total + term
            spectra[(part, energy) + place] = total
        return carry

    lax.fori_loop(0, rows // tall, chunk, 0)


def exchange_kernel(
    groups,
    tiles,
    materials_ref,
    main_ref,
    side_ref,
    out_ref,
    step_ref,
    margin,
    left,
    data,
    spectra,
    margin_sems,
    send_sems,
    recv_sems,
    own_sems,
):
    mesh_ids = pl.DeviceIdType.MESH
    me = lax.axis_index("energy")
    tile = lax.axis_index("tile")
    after = lax.rem(tile + 1, tiles)
    before = lax.rem(tile + tiles - 1, tiles)
    tile_px = main_ref.shape[-1]
    length = side_ref.shape[-1]
    rows = tile_px // groups
    kinds = materials_ref.shape[0] // (2 * groups)
    offsets = sorted(range(1, groups), key=lambda offset: abs(offset - groups // 2))
    peers = {offset: lax.rem(me + offset, groups) for offset in offsets}

    barrier = pltpu.get_barrier_semaphore()
    for neighbour in (after, before):
        pl.semaphore_signal(barrier, inc=1, device_id=(me, neighbour), device_id_type=mesh_ids)
    for offset in offsets:
        pl.semaphore_signal(
            barrier, inc=1, device_id=(peers[offset], tile), device_id_type=mesh_ids
        )

    pl.semaphore_wait(barrier, groups + 1)

    margin_copy = pltpu.make_async_remote_copy(
        src_ref=side_ref,
        dst_ref=margin,
        send_sem=margin_sems.at[0],
        recv_sem=margin_sems.at[1],
        device_id=(me, after),
        device_id_type=mesh_ids,
    )
    margin_copy.start()

    def rows_of(group):
        return pl.ds(pl.multiple_of(group * rows, rows), rows)

    def outward(block):
        columns = pl.ds(block * LANES, LANES)
        source = left if block * LANES < length else main_ref
        copies = [
            pltpu.make_async_remote_copy(
                src_ref=source.at[:, rows_of(peers[offset]), columns],
                dst_ref=data.at[:, me, :, columns],
                send_sem=send_sems.at[0, block, offset],
                recv_sem=recv_sems.at[0, block, offset],
                device_id=(peers[offset], tile),
                device_id_type=mesh_ids,
            )
            for offset in offsets
        ]
        own = pltpu.make_async_copy(
            source.at[:, rows_of(me), columns], data.at[:, me, :, columns], own_sems.at[0, block]
        )
        return copies, own

    def homeward(block):
        columns = pl.ds(block * LANES, LANES)
        copies = [
            pltpu.make_async_remote_copy(
                src_ref=spectra.at[:, peers[offset], :, columns],
                dst_ref=out_ref.at[:, rows_of(me), columns],
                send_sem=send_sems.at[1, block, offset],
                recv_sem=recv_sems.at[1, block, offset],
                device_id=(peers[offset], tile),
                device_id_type=mesh_ids,
            )
            for offset in offsets
        ]
        own = pltpu.make_async_copy(
            spectra.at[:, me, :, columns], out_ref.at[:, rows_of(me), columns], own_sems.at[1, block]
        )
        return copies, own

    def start(moves):
        for copy in moves[0]:
            copy.start()
        moves[1].start()

    blocks = tile_px // LANES
    early = [block for block in range(blocks) if block * LANES >= length]
    late = [block for block in range(blocks) if block * LANES < length]
    going = {}
    for block in early:
        going[block] = outward(block)
        start(going[block])

    gram, trace = fit_scalars(materials_ref, groups, kinds)
    rate = 1.0 / trace
    for one in range(kinds):
        for other in range(kinds):
            unit = 1.0 if one == other else 0.0
            step_ref[one * kinds + other] = unit - rate * gram[one][other]
    margin_copy.wait()
    for block in late:
        columns = slice(block * LANES, (block + 1) * LANES)
        left[:, :, columns] = main_ref[:, :, columns] + margin[:, :, columns]
    for block in late:
        going[block] = outward(block)
        start(going[block])
    coming = {}
    for block in early + late:
        copies, own = going[block]
        for copy in copies:
            copy.wait_recv()
        own.wait()
        fit_columns(
            materials_ref, step_ref, data, spectra, groups, kinds, rate, block * LANES, LANES
        )
        coming[block] = homeward(block)
        start(coming[block])
    for block in early + late:
        for copy in going[block][0]:
            copy.wait_send()
        copies, own = coming[block]
        own.wait()
        for copy in copies:
            copy.wait()


def exchange_fit(main, side, materials):
    groups = lax.axis_size("energy")
    tiles = lax.axis_size("tile")
    tile_px = main.shape[-1]
    length = side.shape[-1]
    kinds = materials.shape[-1]
    rows = tile_px // groups
    blocks = tile_px // LANES
    vmem = pl.BlockSpec(memory_space=pltpu.VMEM)
    return pl.pallas_call(
        functools.partial(exchange_kernel, groups, tiles),
        out_shape=jax.ShapeDtypeStruct(main.shape, jnp.float32),
        in_specs=[pl.BlockSpec(memory_space=pltpu.SMEM), vmem, vmem],
        out_specs=vmem,
        scratch_shapes=[
            pltpu.SMEM((kinds * kinds,), jnp.float32),
            pltpu.VMEM((2, tile_px, length), jnp.float32),
            pltpu.VMEM((2, tile_px, length), jnp.float32),
            pltpu.VMEM((2, groups, rows, tile_px), jnp.float32),
            pltpu.VMEM((2, groups, rows, tile_px), jnp.float32),
            pltpu.SemaphoreType.DMA((2,)),
            pltpu.SemaphoreType.DMA((2, blocks, groups)),
            pltpu.SemaphoreType.DMA((2, blocks, groups)),
            pltpu.SemaphoreType.DMA((2, blocks)),
        ],
        compiler_params=pltpu.CompilerParams(
            collective_id=0, has_side_effects=True, vmem_limit_bytes=32 * 1024 * 1024
        ),
        name="exchange",
    )(materials.reshape(-1), main, side)


def body(object_tiles, probe_wave, measured, positions, materials):
    own_object = object_tiles[0, :, 0]
    tile_px = own_object.shape[-1]
    length = probe_wave.shape[-1]
    tile_count = lax.axis_size("tile")
    row_step = TILE_COLS % tile_count
    fold = row_step == 0
    chunks = [own_object[:, :, at : at + LANES] for at in range(0, length, LANES)]
    strips = [shifted(chunk, "tile", -1) for chunk in chunks]
    lower_strip = None
    if not fold:
        widened = jnp.concatenate(
            [own_object[:, :length]] + [strip[:, :length] for strip in strips], 2
        )
        lower_strip = shifted(widened, "tile", -row_step)
    main, side, below = patch_calls(
        own_object, probe_wave[0], measured[0, 0], positions[0], fold, strips, lower_strip
    )
    if not fold:
        from_above = shifted(below, "tile", row_step)
        main = main.at[:, :length, :].add(from_above[:, :, :tile_px])
        side = side.at[:, :length, :].add(from_above[:, :, tile_px:])
    fitted = exchange_fit(main, side, materials)
    return fitted.reshape(1, 2, 1, tile_px, tile_px)


def solution(mesh):
    in_specs = (
        P("energy", None, "tile", None, None),
        P("energy", None, None, None),
        P("energy", "tile", None, None, None),
        P("tile", None, None),
        P(),
    )
    out_specs = P("energy", None, "tile", None, None)
    return jax.shard_map(body, mesh=mesh, in_specs=in_specs, out_specs=out_specs, check_vma=False)
```

```python
import functools
import math

import jax
import jax.numpy as jnp
import numpy as np
from jax import lax
from jax.experimental import pallas as pl
from jax.experimental.pallas import tpu as pltpu
from jax.sharding import PartitionSpec as P

TILE_COLS = 4
FIT_STEPS = 10
LANES = 128
VMEM_LIMIT = 12 * 1024 * 1024
LOAD_LIMIT = 8 * 1024 * 1024


amplitude_floor = 0.5


def shifted(value, axis, steps):
    count = lax.axis_size(axis)
    pairs = [(source, (source + steps) % count) for source in range(count)]
    return lax.ppermute(value, axis, pairs)


def trig_parts(rows, columns, length):
    angles = 2.0 * math.pi / length * (rows[:, None] * columns[None, :] % length)
    return np.stack([np.cos(angles), np.sin(angles)]).astype(np.float32).astype(jnp.bfloat16)


def fourier_parts(length):
    counter = np.arange(length, dtype=np.int64)
    half = counter[: length // 2]
    left = np.stack([trig_parts(half, counter[parity::2], length) for parity in range(2)])
    return jnp.asarray(left), jnp.asarray(trig_parts(counter, counter, length))


def joined(top_left, top_right, bottom_left, bottom_right):
    return jnp.concatenate(
        [
            jnp.concatenate([top_left, top_right], 1),
            jnp.concatenate([bottom_left, bottom_right], 1),
        ],
        0,
    )


def transform(even, odd, left_ref, right_ref):
    length = even.shape[0]
    half = length // 2
    one = jnp.dot(left_ref[0], even, preferred_element_type=jnp.float32)
    two = jnp.dot(left_ref[1], odd, preferred_element_type=jnp.float32)
    upper = (one + two).astype(jnp.bfloat16)
    lower = (one - two).astype(jnp.bfloat16)
    beside = joined(upper[:half], upper[half:], lower[:half], lower[half:])
    outer = jnp.dot(beside, right_ref[...], preferred_element_type=jnp.float32)
    return outer[:, :length], outer[:, length:]


def window(ref, part, rows, block, shift, length):
    lane = lax.broadcasted_iota(jnp.int32, (rows.size, LANES), 1)
    back = lax.rem(LANES - shift, LANES)
    tiles = [
        pltpu.roll(ref[part, block + at, rows, :], back, 1) for at in range(length // LANES + 1)
    ]
    keep = lane < LANES - shift
    return jnp.concatenate(
        [jnp.where(keep, one, other) for one, other in zip(tiles[:-1], tiles[1:])], 1
    )


def add_window(ref, part, row, block, shift, term):
    length = term.shape[0]
    lane = lax.broadcasted_iota(jnp.int32, (length, LANES), 1)
    tiles = [pltpu.roll(term[:, at : at + LANES], shift, 1) for at in range(0, length, LANES)]
    keep = lane >= shift
    zero = jnp.zeros_like(tiles[0])
    for at, (one, other) in enumerate(zip(tiles + [zero], [zero] + tiles)):
        place = (part, block + at, pl.ds(row, length), slice(None))
        ref[place] = ref[place] + jnp.where(keep, one, other)


def load_kernel(fold, object_ref, probe_ref, left_ref, right_ref, *refs):
    *strips, gradient, field, terms, left, right, probe, split = refs[:-3]
    parts_left, parts_right, sems = refs[-3:]
    length = probe_ref.shape[-1]
    half = length // 2
    pieces = length // LANES
    tile_px = object_ref.shape[-1]
    top = pl.ds(0, tile_px)
    bottom = pl.ds(tile_px, length)
    moves = [(left_ref, parts_left), (right_ref, parts_right)]
    for piece, strip in enumerate(strips):
        moves.append((object_ref.at[:, :, pl.ds(piece * LANES, LANES)], strip))
    for piece in range(pieces):
        columns = pl.ds(piece * LANES, LANES)
        moves.append((probe_ref.at[:, :, columns], probe.at[:, piece]))
    for block in range(tile_px // LANES):
        columns = pl.ds(block * LANES, LANES)
        moves.append((object_ref.at[:, :, columns], field.at[:, block, top, :]))
        if fold:
            source = object_ref.at[:, pl.ds(0, length), columns]
            moves.append((source, field.at[:, block, bottom, :]))
    copies = [
        pltpu.make_async_copy(source, target, sems.at[number])
        for number, (source, target) in enumerate(moves)
    ]
    for copy in copies:
        copy.start()
    gradient[...] = jnp.zeros_like(gradient)
    terms[...] = jnp.zeros_like(terms)
    for copy in copies[:2]:
        copy.wait()
    for parity in range(2):
        cosine = parts_left[parity, 0]
        sine = parts_left[parity, 1]
        left[0, parity] = joined(cosine, sine, -sine, cosine)
        left[1, parity] = joined(cosine, -sine, sine, cosine)
    scale = jnp.asarray(1.0 / length, jnp.bfloat16)
    cosine = parts_right[0] * scale
    sine = parts_right[1] * scale
    right[0] = joined(cosine, -sine, sine, cosine)
    right[1] = joined(cosine, sine, -sine, cosine)
    early = 2 + len(strips) + pieces
    for copy in copies[2:early]:
        copy.wait()
    for parity in range(2):
        for part in range(2):
            for piece in range(pieces):
                columns = slice(piece * LANES, (piece + 1) * LANES)
                rows = pl.ds(parity, half, stride=2)
                split[parity, part, :, columns] = probe[part, piece, rows, :]
    for copy in copies[early:]:
        copy.wait()


def patch_kernel(fold, phase, phases, *refs):
    first = phase == 0
    last = phase == phases - 1
    lower_count = 1 if last and not fold else 0
    strip_count = 0 if first else 1
    lead = 1 + lower_count + strip_count
    corners_ref = refs[0]
    strip_ref = None if first else refs[1]
    lower_ref = refs[2] if lower_count else None
    held, left, right, probe, split = refs[lead : lead + 5]
    refs = refs[lead + 5 + (3 if first else 5) :]
    gradient, field, terms, wave, change = refs[:5]
    order, sems = refs[-2:]
    length = wave.shape[-1]
    half = length // 2
    pieces = length // LANES
    width = field.shape[1]
    blocks = width - pieces
    tile_px = blocks * LANES
    count = held.shape[0]
    limit = tile_px - length
    top = pl.ds(0, tile_px)
    bottom = pl.ds(tile_px, length)
    moves = []
    if not first:
        block = blocks + phase - 1
        moves.append((strip_ref, field.at[:, block, top, :]))
        if fold:
            moves.append((strip_ref.at[:, pl.ds(0, length), :], field.at[:, block, bottom, :]))
        elif last:
            for block in range(width):
                columns = pl.ds(block * LANES, LANES)
                moves.append((lower_ref.at[:, :, columns], field.at[:, block, bottom, :]))
    copies = [
        pltpu.make_async_copy(source, target, sems.at[number])
        for number, (source, target) in enumerate(moves)
    ]
    for copy in copies:
        copy.start()

    def rank(number):
        beyond = corners_ref[1, number] - limit
        kind = sum((beyond > step * LANES).astype(jnp.int32) for step in range(phases - 1))
        if not fold:
            kind = jnp.where(corners_ref[0, number] > limit, phases - 1, kind)
        return kind

    kinds = [rank(number) for number in range(count)]
    ends = [
        sum((kind <= step).astype(jnp.int32) for kind in kinds) for step in range(phases)
    ]
    place = [jnp.int32(0)] + ends[:-1]
    for number, kind in enumerate(kinds):
        spot = place[-1]
        for step in range(phases - 1):
            spot = jnp.where(kind == step, place[step], spot)
        order[spot] = number
        place = [
            value + (kind == step).astype(jnp.int32) for step, value in enumerate(place)
        ]
    begin = jnp.maximum(ends[phase - 1] - 2, 0) if phase else 0
    end = count - 1 if last else jnp.maximum(ends[phase] - 2, 0)
    for copy in copies:
        copy.wait()

    def corner(turn):
        number = order[turn]
        row = corners_ref[0, number]
        col = corners_ref[1, number]
        block = col // LANES
        return number, row, block, col - block * LANES

    def gather(turn):
        _, row, block, shift = corner(turn)
        for parity in range(2):
            rows = pl.ds(row + parity, half, stride=2)
            piece_real = window(field, 0, rows, block, shift, length)
            piece_imag = window(field, 1, rows, block, shift, length)
            probe_real = split[parity, 0]
            probe_imag = split[parity, 1]
            exit_real = probe_real * piece_real - probe_imag * piece_imag
            exit_imag = probe_real * piece_imag + probe_imag * piece_real
            wave[parity, :half, :] = exit_real.astype(jnp.bfloat16)
            wave[parity, half:, :] = exit_imag.astype(jnp.bfloat16)

    def scatter(turn):
        _, row, block, shift = corner(turn)
        add_window(gradient, 0, row, block, shift, terms[0])
        add_window(gradient, 1, row, block, shift, terms[1])

    def outward(turn):
        far_real, far_imag = transform(wave[0], wave[1], left.at[0], right.at[0])
        square = far_real * far_real + far_imag * far_imag
        scale = lax.rsqrt(jnp.maximum(square, amplitude_floor * amplitude_floor))
        factor = held[order[turn]].astype(jnp.float32) * scale - 1.0
        return factor * far_real, factor * far_imag

    def keep(parts):
        for part in range(2):
            for piece in range(pieces):
                change[part, piece] = parts[part][:, piece * LANES : (piece + 1) * LANES]

    def changed(parity):
        rows = pl.ds(parity, half, stride=2)
        return jnp.concatenate(
            [
                jnp.concatenate([change[part, piece, rows, :] for piece in range(pieces)], 1)
                for part in range(2)
            ],
            0,
        ).astype(jnp.bfloat16)

    def homeward():
        back_real, back_imag = transform(changed(0), changed(1), left.at[1], right.at[1])
        probe_real = jnp.concatenate([probe[0, piece] for piece in range(pieces)], 1)
        probe_imag = jnp.concatenate([probe[1, piece] for piece in range(pieces)], 1)
        return (
            probe_real * back_real + probe_imag * back_imag,
            probe_real * back_imag - probe_imag * back_real,
        )

    def step(turn, carry):
        scatter(jnp.maximum(turn - 1, 0))
        parts = outward(turn + 1)
        back = homeward()
        keep(parts)
        gather(jnp.minimum(turn + 2, count - 1))
        terms[0] = back[0]
        terms[1] = back[1]
        return carry

    ready = ends[phase] >= 2
    if not first:
        ready = jnp.logical_and(ready, ends[phase - 1] < 2)

    @pl.when(ready)
    def _():
        gather(0)
        keep(outward(0))
        gather(1)

    lax.fori_loop(begin, end, step, 0)
    if last:
        scatter(count - 2)
        back = homeward()
        terms[0] = back[0]
        terms[1] = back[1]
        scatter(count - 1)


def patch_calls(own_object, probe, measured, corners, fold, shift):
    tile_px = own_object.shape[-1]
    length = probe.shape[-1]
    count = measured.shape[0]
    width = tile_px + length
    pieces = length // LANES
    phases = 1 + pieces
    vmem = pl.BlockSpec(memory_space=pltpu.VMEM)
    anywhere = pl.BlockSpec(memory_space=pl.ANY)
    smem = pl.BlockSpec(memory_space=pltpu.SMEM)

    def single(*shape):
        return jax.ShapeDtypeStruct(shape, jnp.float32)

    def brief(*shape):
        return jax.ShapeDtypeStruct(shape, jnp.bfloat16)

    sums = (2, width // LANES, width, LANES)
    moving = [
        single(*sums),
        single(*sums),
        single(2, length, length),
        brief(2, length, length),
        single(2, pieces, length, LANES),
    ]
    fixed = [
        brief(2, 2, length, length),
        brief(2, 2 * length, 2 * length),
        single(2, pieces, length, LANES),
        single(2, 2, length // 2, length),
    ]
    loaded = [single(2, tile_px, LANES)] * pieces + moving[:3] + fixed
    parts_left, parts_right = fourier_parts(length)
    sources = (own_object, probe, parts_left, parts_right)
    out = pl.pallas_call(
        functools.partial(load_kernel, fold),
        out_shape=loaded,
        in_specs=[anywhere] * 4,
        out_specs=[vmem] * len(loaded),
        scratch_shapes=[
            pltpu.VMEM(parts_left.shape, jnp.bfloat16),
            pltpu.VMEM(parts_right.shape, jnp.bfloat16),
            pltpu.SemaphoreType.DMA((2 + 2 * pieces + 2 * (tile_px // LANES),)),
        ],
        compiler_params=pltpu.CompilerParams(vmem_limit_bytes=LOAD_LIMIT),
        cost_estimate=pl.CostEstimate(flops=10**10, bytes_accessed=2**24, transcendentals=0),
        name="load",
    )(*(pltpu.with_memory_space_constraint(value, pltpu.HBM) for value in sources))
    strips = [shift(strip) for strip in out[:pieces]]
    state = list(out[pieces : pieces + 3])
    held = [measured, *out[pieces + 3 :]]
    for phase in range(phases):
        last = phase == phases - 1
        more = [strips[phase - 1]] if phase else []
        if last and not fold:
            widened = jnp.concatenate(
                [own_object[:, :length]] + [strip[:, :length] for strip in strips], 2
            )
            more.append(shifted(widened, "tile", -(TILE_COLS % lax.axis_size("tile"))))
        lead = 1 + len(more) + len(held)
        state = pl.pallas_call(
            functools.partial(patch_kernel, fold, phase, phases),
            out_shape=moving,
            in_specs=[smem] + [anywhere] * len(more) + [vmem] * (len(held) + len(state)),
            out_specs=[vmem] * len(moving),
            scratch_shapes=[
                pltpu.SMEM((count,), jnp.int32),
                pltpu.SemaphoreType.DMA((2 + width // LANES,)),
            ],
            input_output_aliases={lead + at: at for at in range(len(state))},
            compiler_params=pltpu.CompilerParams(vmem_limit_bytes=VMEM_LIMIT),
            cost_estimate=pl.CostEstimate(
                flops=8 * count * length**3,
                bytes_accessed=8 * tile_px * tile_px,
                transcendentals=0,
            ),
            name=f"patches_{phase}",
        )(corners, *more, *held, *state)
    return state[0], state[1], held[3]


def fit_scalars(materials_ref, energies, kinds):
    spectra = [
        [materials_ref[part, energy, kind] for kind in range(kinds)]
        for part in range(2)
        for energy in range(energies)
    ]
    gram = [[None] * kinds for _ in range(kinds)]
    for one in range(kinds):
        for other in range(one, kinds):
            total = spectra[0][one] * spectra[0][other]
            for row in spectra[1:]:
                total = total + row[one] * row[other]
            gram[one][other] = total
            gram[other][one] = total
    trace = gram[0][0]
    for one in range(1, kinds):
        trace = trace + gram[one][one]
    return gram, trace


def fit_columns(materials_ref, step_ref, data, spectra, energies, kinds, rate, begin, wide):
    rows = data.shape[2]
    tall = 16 if rows % 16 == 0 else 8
    pairs = [(part, energy) for part in range(2) for energy in range(energies)]

    def chunk(number, carry):
        row = pl.multiple_of(number * tall, tall)
        place = (pl.ds(row, tall), pl.ds(begin, wide))
        target = [None] * kinds
        for part, energy in pairs:
            plane = data[(part, energy) + place]
            for kind in range(kinds):
                term = materials_ref[part, energy, kind] * plane
                target[kind] = term if target[kind] is None else target[kind] + term
        target = [rate * value for value in target]
        current = [jnp.maximum(value, 0.0) for value in target]

        def descend(turn, current):
            following = []
            for one in range(kinds):
                total = target[one]
                for other in range(kinds):
                    total = total + step_ref[one * kinds + other] * current[other]
                following.append(jnp.maximum(total, 0.0))
            return following

        current = lax.fori_loop(1, FIT_STEPS, descend, current)
        for part, energy in pairs:
            total = None
            for kind in range(kinds):
                term = materials_ref[part, energy, kind] * current[kind]
                total = term if total is None else total + term
            spectra[(part, energy) + place] = total
        return carry

    lax.fori_loop(0, rows // tall, chunk, 0)


def exchange_kernel(
    groups,
    tiles,
    fold,
    materials_ref,
    gradient,
    field,
    probe,
    out_ref,
    step_ref,
    main,
    side,
    margin,
    data,
    spectra,
    margin_sems,
    send_sems,
    recv_sems,
    own_sems,
):
    mesh_ids = pl.DeviceIdType.MESH
    me = lax.axis_index("energy")
    tile = lax.axis_index("tile")
    after = lax.rem(tile + 1, tiles)
    before = lax.rem(tile + tiles - 1, tiles)
    tile_px = out_ref.shape[-1]
    length = probe.shape[2]
    blocks = tile_px // LANES
    rows = tile_px // groups
    kinds = materials_ref.shape[2]
    offsets = sorted(range(1, groups), key=lambda offset: abs(offset - groups // 2))
    peers = {offset: lax.rem(me + offset, groups) for offset in offsets}

    barrier = pltpu.get_barrier_semaphore()
    for neighbour in (after, before):
        pl.semaphore_signal(barrier, inc=1, device_id=(me, neighbour), device_id_type=mesh_ids)
    for offset in offsets:
        pl.semaphore_signal(
            barrier, inc=1, device_id=(peers[offset], tile), device_id_type=mesh_ids
        )

    peak = jnp.max(probe[0] * probe[0] + probe[1] * probe[1])
    tall = 64
    inverse = 1.0 / jnp.full((tall, LANES), peak, jnp.float32)

    def finish(wrapped, number, carry):
        place = (pl.ds(pl.multiple_of(number * tall, tall), tall), slice(None))
        beyond = pl.ds(pl.multiple_of(tile_px + number * tall, tall), tall)
        for part in range(2):
            for block in range(field.shape[1]):
                value = gradient[(part, block) + place]
                if wrapped:
                    value = value + gradient[part, block, beyond, :]
                share = value * inverse
                if block < blocks:
                    main[(part, block) + place] = field[(part, block) + place] + share
                else:
                    side[(part, block - blocks) + place] = share
        return carry

    lax.fori_loop(0, length // tall, functools.partial(finish, fold), 0)
    lax.fori_loop(length // tall, tile_px // tall, functools.partial(finish, False), 0)

    pl.semaphore_wait(barrier, groups + 1)

    margin_copy = pltpu.make_async_remote_copy(
        src_ref=side,
        dst_ref=margin,
        send_sem=margin_sems.at[0],
        recv_sem=margin_sems.at[1],
        device_id=(me, after),
        device_id_type=mesh_ids,
    )
    margin_copy.start()

    def rows_of(group):
        return pl.ds(pl.multiple_of(group * rows, rows), rows)

    def outward(block):
        columns = pl.ds(block * LANES, LANES)
        copies = [
            pltpu.make_async_remote_copy(
                src_ref=main.at[:, block, rows_of(peers[offset]), :],
                dst_ref=data.at[:, me, :, columns],
                send_sem=send_sems.at[0, block, offset],
                recv_sem=recv_sems.at[0, block, offset],
                device_id=(peers[offset], tile),
                device_id_type=mesh_ids,
            )
            for offset in offsets
        ]
        own = pltpu.make_async_copy(
            main.at[:, block, rows_of(me), :], data.at[:, me, :, columns], own_sems.at[0, block]
        )
        return copies, own

    def homeward(block):
        columns = pl.ds(block * LANES, LANES)
        copies = [
            pltpu.make_async_remote_copy(
                src_ref=spectra.at[:, peers[offset], :, columns],
                dst_ref=out_ref.at[:, rows_of(me), columns],
                send_sem=send_sems.at[1, block, offset],
                recv_sem=recv_sems.at[1, block, offset],
                device_id=(peers[offset], tile),
                device_id_type=mesh_ids,
            )
            for offset in offsets
        ]
        own = pltpu.make_async_copy(
            spectra.at[:, me, :, columns], out_ref.at[:, rows_of(me), columns], own_sems.at[1, block]
        )
        return copies, own

    def start(moves):
        for copy in moves[0]:
            copy.start()
        moves[1].start()

    early = [block for block in range(blocks) if block * LANES >= length]
    late = [block for block in range(blocks) if block * LANES < length]
    going = {}
    for block in early:
        going[block] = outward(block)
        start(going[block])

    gram, trace = fit_scalars(materials_ref, groups, kinds)
    rate = 1.0 / trace
    for one in range(kinds):
        for other in range(kinds):
            unit = 1.0 if one == other else 0.0
            step_ref[one * kinds + other] = unit - rate * gram[one][other]
    margin_copy.wait()
    for block in late:
        main[:, block] = main[:, block] + margin[:, block]
    for block in late:
        going[block] = outward(block)
        start(going[block])
    coming = {}
    for block in early + late:
        copies, own = going[block]
        for copy in copies:
            copy.wait_recv()
        own.wait()
        fit_columns(
            materials_ref, step_ref, data, spectra, groups, kinds, rate, block * LANES, LANES
        )
        coming[block] = homeward(block)
        start(coming[block])
    for block in early + late:
        for copy in going[block][0]:
            copy.wait_send()
        copies, own = coming[block]
        own.wait()
        for copy in copies:
            copy.wait()


def exchange_fit(gradient, field, probe, materials, fold):
    groups = lax.axis_size("energy")
    tiles = lax.axis_size("tile")
    pieces = probe.shape[1]
    blocks = field.shape[1] - pieces
    tile_px = blocks * LANES
    kinds = materials.shape[-1]
    rows = tile_px // groups
    vmem = pl.BlockSpec(memory_space=pltpu.VMEM)
    return pl.pallas_call(
        functools.partial(exchange_kernel, groups, tiles, fold),
        out_shape=jax.ShapeDtypeStruct((2, tile_px, tile_px), jnp.float32),
        in_specs=[pl.BlockSpec(memory_space=pltpu.SMEM), vmem, vmem, vmem],
        out_specs=vmem,
        scratch_shapes=[
            pltpu.SMEM((kinds * kinds,), jnp.float32),
            pltpu.VMEM((2, blocks, tile_px, LANES), jnp.float32),
            pltpu.VMEM((2, pieces, tile_px, LANES), jnp.float32),
            pltpu.VMEM((2, pieces, tile_px, LANES), jnp.float32),
            pltpu.VMEM((2, groups, rows, tile_px), jnp.float32),
            pltpu.VMEM((2, groups, rows, tile_px), jnp.float32),
            pltpu.SemaphoreType.DMA((2,)),
            pltpu.SemaphoreType.DMA((2, blocks, groups)),
            pltpu.SemaphoreType.DMA((2, blocks, groups)),
            pltpu.SemaphoreType.DMA((2, blocks)),
        ],
        compiler_params=pltpu.CompilerParams(
            collective_id=0, has_side_effects=True, vmem_limit_bytes=24 * 1024 * 1024
        ),
        name="exchange",
    )(materials, gradient, field, probe)


def body(object_tiles, probe_wave, measured, positions, materials):
    own_object = object_tiles[0, :, 0]
    tile_px = own_object.shape[-1]
    length = probe_wave.shape[-1]
    row_step = TILE_COLS % lax.axis_size("tile")
    fold = row_step == 0
    gradient, field, probe = patch_calls(
        own_object,
        probe_wave[0],
        measured[0, 0],
        positions[0].T,
        fold,
        functools.partial(shifted, axis="tile", steps=-1),
    )
    if not fold:
        from_above = shifted(gradient[:, :, tile_px:], "tile", row_step)
        gradient = gradient.at[:, :, :length].add(from_above)
    fitted = exchange_fit(gradient, field, probe, materials, fold)
    return fitted.reshape(1, 2, 1, tile_px, tile_px)


def solution(mesh):
    in_specs = (
        P("energy", None, "tile", None, None),
        P("energy", None, None, None),
        P("energy", "tile", None, None, None),
        P("tile", None, None),
        P(),
    )
    out_specs = P("energy", None, "tile", None, None)
    return jax.shard_map(body, mesh=mesh, in_specs=in_specs, out_specs=out_specs, check_vma=False)
```

```python
import functools
import math

import jax
import jax.numpy as jnp
import numpy as np
from jax import lax
from jax.experimental import pallas as pl
from jax.experimental.pallas import tpu as pltpu
from jax.sharding import PartitionSpec as P

TILE_COLS = 4
FIT_STEPS = 10
LANES = 128
VMEM_LIMIT = 12 * 1024 * 1024
LOAD_LIMIT = 8 * 1024 * 1024


amplitude_floor = 0.5


def shifted(value, axis, steps):
    count = lax.axis_size(axis)
    pairs = [(source, (source + steps) % count) for source in range(count)]
    return lax.ppermute(value, axis, pairs)


def trig_parts(rows, columns, length):
    angles = 2.0 * math.pi / length * (rows[:, None] * columns[None, :] % length)
    return np.stack([np.cos(angles), np.sin(angles)]).astype(np.float32).astype(jnp.bfloat16)


def fourier_parts(length):
    counter = np.arange(length, dtype=np.int64)
    half = counter[: length // 2]
    left = np.stack([trig_parts(half, counter[parity::2], length) for parity in range(2)])
    return jnp.asarray(left), jnp.asarray(trig_parts(counter, counter, length))


def joined(top_left, top_right, bottom_left, bottom_right):
    return jnp.concatenate(
        [
            jnp.concatenate([top_left, top_right], 1),
            jnp.concatenate([bottom_left, bottom_right], 1),
        ],
        0,
    )


def transform(even, odd, left_ref, right_ref):
    length = even.shape[0]
    half = length // 2
    one = jnp.dot(left_ref[0], even, preferred_element_type=jnp.float32)
    two = jnp.dot(left_ref[1], odd, preferred_element_type=jnp.float32)
    upper = (one + two).astype(jnp.bfloat16)
    lower = (one - two).astype(jnp.bfloat16)
    beside = joined(upper[:half], upper[half:], lower[:half], lower[half:])
    outer = jnp.dot(beside, right_ref[...], preferred_element_type=jnp.float32)
    return outer[:, :length], outer[:, length:]


def window(ref, part, rows, block, shift, length):
    lane = lax.broadcasted_iota(jnp.int32, (rows.size, LANES), 1)
    back = lax.rem(LANES - shift, LANES)
    tiles = [
        pltpu.roll(ref[part, block + at, rows, :], back, 1) for at in range(length // LANES + 1)
    ]
    keep = lane < LANES - shift
    return jnp.concatenate(
        [jnp.where(keep, one, other) for one, other in zip(tiles[:-1], tiles[1:])], 1
    )


def add_window(ref, part, row, block, shift, term):
    length = term.shape[0]
    lane = lax.broadcasted_iota(jnp.int32, (length, LANES), 1)
    tiles = [pltpu.roll(term[:, at : at + LANES], shift, 1) for at in range(0, length, LANES)]
    keep = lane >= shift
    zero = jnp.zeros_like(tiles[0])
    for at, (one, other) in enumerate(zip(tiles + [zero], [zero] + tiles)):
        place = (part, block + at, pl.ds(row, length), slice(None))
        ref[place] = ref[place] + jnp.where(keep, one, other)


def load_kernel(object_ref, probe_ref, left_ref, right_ref, *refs):
    *strips, gradient, terms, left, right, probe, split = refs[:-3]
    parts_left, parts_right, sems = refs[-3:]
    length = probe_ref.shape[-1]
    half = length // 2
    pieces = length // LANES
    moves = [(left_ref, parts_left), (right_ref, parts_right)]
    for piece, strip in enumerate(strips):
        moves.append((object_ref.at[:, :, pl.ds(piece * LANES, LANES)], strip))
    for piece in range(pieces):
        columns = pl.ds(piece * LANES, LANES)
        moves.append((probe_ref.at[:, :, columns], probe.at[:, piece]))
    copies = [
        pltpu.make_async_copy(source, target, sems.at[number])
        for number, (source, target) in enumerate(moves)
    ]
    for copy in copies:
        copy.start()
    gradient[...] = jnp.zeros_like(gradient)
    terms[...] = jnp.zeros_like(terms)
    for copy in copies[:2]:
        copy.wait()
    for parity in range(2):
        cosine = parts_left[parity, 0]
        sine = parts_left[parity, 1]
        left[0, parity] = joined(cosine, sine, -sine, cosine)
        left[1, parity] = joined(cosine, -sine, sine, cosine)
    scale = jnp.asarray(1.0 / length, jnp.bfloat16)
    cosine = parts_right[0] * scale
    sine = parts_right[1] * scale
    right[0] = joined(cosine, -sine, sine, cosine)
    right[1] = joined(cosine, sine, -sine, cosine)
    for copy in copies[2:]:
        copy.wait()
    for parity in range(2):
        for part in range(2):
            for piece in range(pieces):
                columns = slice(piece * LANES, (piece + 1) * LANES)
                rows = pl.ds(parity, half, stride=2)
                split[parity, part, :, columns] = probe[part, piece, rows, :]


def patch_kernel(fold, phase, phases, *refs):
    first = phase == 0
    last = phase == phases - 1
    lower_count = 1 if last and not fold else 0
    lead = 2 + lower_count
    corners_ref = refs[0]
    source_ref = refs[1]
    lower_ref = refs[2] if lower_count else None
    held, left, right, probe, split = refs[lead : lead + 5]
    refs = refs[lead + 5 + (2 if first else 5) :]
    gradient, terms, field, wave, change = refs[:5]
    order, sems = refs[-2:]
    length = wave.shape[-1]
    half = length // 2
    pieces = length // LANES
    width = field.shape[1]
    blocks = width - pieces
    tile_px = blocks * LANES
    count = held.shape[0]
    limit = tile_px - length
    top = pl.ds(0, tile_px)
    bottom = pl.ds(tile_px, length)
    moves = []
    if first:
        for block in range(blocks):
            columns = pl.ds(block * LANES, LANES)
            moves.append((source_ref.at[:, :, columns], field.at[:, block, top, :]))
            if fold:
                source = source_ref.at[:, pl.ds(0, length), columns]
                moves.append((source, field.at[:, block, bottom, :]))
    else:
        block = blocks + phase - 1
        moves.append((source_ref, field.at[:, block, top, :]))
        if fold:
            moves.append((source_ref.at[:, pl.ds(0, length), :], field.at[:, block, bottom, :]))
        elif last:
            for block in range(width):
                columns = pl.ds(block * LANES, LANES)
                moves.append((lower_ref.at[:, :, columns], field.at[:, block, bottom, :]))
    copies = [
        pltpu.make_async_copy(source, target, sems.at[number])
        for number, (source, target) in enumerate(moves)
    ]
    for copy in copies:
        copy.start()

    def rank(number):
        beyond = corners_ref[1, number] - limit
        kind = sum((beyond > step * LANES).astype(jnp.int32) for step in range(phases - 1))
        if not fold:
            kind = jnp.where(corners_ref[0, number] > limit, phases - 1, kind)
        return kind

    kinds = [rank(number) for number in range(count)]
    ends = [
        sum((kind <= step).astype(jnp.int32) for kind in kinds) for step in range(phases)
    ]
    place = [jnp.int32(0)] + ends[:-1]
    for number, kind in enumerate(kinds):
        spot = place[-1]
        for step in range(phases - 1):
            spot = jnp.where(kind == step, place[step], spot)
        order[spot] = number
        place = [
            value + (kind == step).astype(jnp.int32) for step, value in enumerate(place)
        ]
    begin = jnp.maximum(ends[phase - 1] - 2, 0) if phase else 0
    end = count - 1 if last else jnp.maximum(ends[phase] - 2, 0)
    for copy in copies:
        copy.wait()

    def corner(turn):
        number = order[turn]
        row = corners_ref[0, number]
        col = corners_ref[1, number]
        block = col // LANES
        return number, row, block, col - block * LANES

    def gather(turn):
        _, row, block, shift = corner(turn)
        for parity in range(2):
            rows = pl.ds(row + parity, half, stride=2)
            piece_real = window(field, 0, rows, block, shift, length)
            piece_imag = window(field, 1, rows, block, shift, length)
            probe_real = split[parity, 0]
            probe_imag = split[parity, 1]
            exit_real = probe_real * piece_real - probe_imag * piece_imag
            exit_imag = probe_real * piece_imag + probe_imag * piece_real
            wave[parity, :half, :] = exit_real.astype(jnp.bfloat16)
            wave[parity, half:, :] = exit_imag.astype(jnp.bfloat16)

    def scatter(turn):
        _, row, block, shift = corner(turn)
        add_window(gradient, 0, row, block, shift, terms[0])
        add_window(gradient, 1, row, block, shift, terms[1])

    def outward(turn):
        far_real, far_imag = transform(wave[0], wave[1], left.at[0], right.at[0])
        square = far_real * far_real + far_imag * far_imag
        scale = lax.rsqrt(jnp.maximum(square, amplitude_floor * amplitude_floor))
        factor = held[order[turn]].astype(jnp.float32) * scale - 1.0
        return factor * far_real, factor * far_imag

    def keep(parts):
        for part in range(2):
            for piece in range(pieces):
                change[part, piece] = parts[part][:, piece * LANES : (piece + 1) * LANES]

    def changed(parity):
        rows = pl.ds(parity, half, stride=2)
        return jnp.concatenate(
            [
                jnp.concatenate([change[part, piece, rows, :] for piece in range(pieces)], 1)
                for part in range(2)
            ],
            0,
        ).astype(jnp.bfloat16)

    def homeward():
        back_real, back_imag = transform(changed(0), changed(1), left.at[1], right.at[1])
        probe_real = jnp.concatenate([probe[0, piece] for piece in range(pieces)], 1)
        probe_imag = jnp.concatenate([probe[1, piece] for piece in range(pieces)], 1)
        return (
            probe_real * back_real + probe_imag * back_imag,
            probe_real * back_imag - probe_imag * back_real,
        )

    def step(turn, carry):
        scatter(jnp.maximum(turn - 1, 0))
        parts = outward(turn + 1)
        back = homeward()
        keep(parts)
        gather(jnp.minimum(turn + 2, count - 1))
        terms[0] = back[0]
        terms[1] = back[1]
        return carry

    ready = ends[phase] >= 2
    if not first:
        ready = jnp.logical_and(ready, ends[phase - 1] < 2)

    @pl.when(ready)
    def _():
        gather(0)
        keep(outward(0))
        gather(1)

    lax.fori_loop(begin, end, step, 0)
    if last:
        scatter(count - 2)
        back = homeward()
        terms[0] = back[0]
        terms[1] = back[1]
        scatter(count - 1)


def patch_calls(own_object, probe, measured, corners, fold, shift):
    tile_px = own_object.shape[-1]
    length = probe.shape[-1]
    count = measured.shape[0]
    width = tile_px + length
    pieces = length // LANES
    phases = 1 + pieces
    vmem = pl.BlockSpec(memory_space=pltpu.VMEM)
    anywhere = pl.BlockSpec(memory_space=pl.ANY)
    smem = pl.BlockSpec(memory_space=pltpu.SMEM)

    def single(*shape):
        return jax.ShapeDtypeStruct(shape, jnp.float32)

    def brief(*shape):
        return jax.ShapeDtypeStruct(shape, jnp.bfloat16)

    sums = (2, width // LANES, width, LANES)
    moving = [
        single(*sums),
        single(2, length, length),
        single(*sums),
        brief(2, length, length),
        single(2, pieces, length, LANES),
    ]
    fixed = [
        brief(2, 2, length, length),
        brief(2, 2 * length, 2 * length),
        single(2, pieces, length, LANES),
        single(2, 2, length // 2, length),
    ]
    loaded = [single(2, tile_px, LANES)] * pieces + moving[:2] + fixed
    parts_left, parts_right = fourier_parts(length)
    sources = (own_object, probe, parts_left, parts_right)
    out = pl.pallas_call(
        load_kernel,
        out_shape=loaded,
        in_specs=[anywhere] * 4,
        out_specs=[vmem] * len(loaded),
        scratch_shapes=[
            pltpu.VMEM(parts_left.shape, jnp.bfloat16),
            pltpu.VMEM(parts_right.shape, jnp.bfloat16),
            pltpu.SemaphoreType.DMA((2 + 2 * pieces,)),
        ],
        compiler_params=pltpu.CompilerParams(vmem_limit_bytes=LOAD_LIMIT),
        cost_estimate=pl.CostEstimate(flops=10**10, bytes_accessed=2**24, transcendentals=0),
        name="load",
    )(*(pltpu.with_memory_space_constraint(value, pltpu.HBM) for value in sources))
    strips = [shift(strip) for strip in out[:pieces]]
    state = list(out[pieces : pieces + 2])
    held = [measured, *out[pieces + 2 :]]
    for phase in range(phases):
        last = phase == phases - 1
        more = [strips[phase - 1] if phase else own_object]
        if last and not fold:
            widened = jnp.concatenate(
                [own_object[:, :length]] + [strip[:, :length] for strip in strips], 2
            )
            more.append(shifted(widened, "tile", -(TILE_COLS % lax.axis_size("tile"))))
        lead = 1 + len(more) + len(held)
        state = pl.pallas_call(
            functools.partial(patch_kernel, fold, phase, phases),
            out_shape=moving,
            in_specs=[smem] + [anywhere] * len(more) + [vmem] * (len(held) + len(state)),
            out_specs=[vmem] * len(moving),
            scratch_shapes=[
                pltpu.SMEM((count,), jnp.int32),
                pltpu.SemaphoreType.DMA((2 * (width // LANES),)),
            ],
            input_output_aliases={lead + at: at for at in range(len(state))},
            compiler_params=pltpu.CompilerParams(
                vmem_limit_bytes=VMEM_LIMIT
            ),
            cost_estimate=pl.CostEstimate(
                flops=8 * count * length**3,
                bytes_accessed=8 * tile_px * tile_px,
                transcendentals=0,
            ),
            name=f"patches_{phase}",
        )(corners, *more, *held, *state)
    return state[0], state[2], held[3]


def fit_scalars(materials_ref, energies, kinds):
    spectra = [
        [materials_ref[part, energy, kind] for kind in range(kinds)]
        for part in range(2)
        for energy in range(energies)
    ]
    gram = [[None] * kinds for _ in range(kinds)]
    for one in range(kinds):
        for other in range(one, kinds):
            total = spectra[0][one] * spectra[0][other]
            for row in spectra[1:]:
                total = total + row[one] * row[other]
            gram[one][other] = total
            gram[other][one] = total
    trace = gram[0][0]
    for one in range(1, kinds):
        trace = trace + gram[one][one]
    return gram, trace


def fit_columns(materials_ref, step_ref, data, spectra, energies, kinds, rate, begin, wide):
    rows = data.shape[2]
    tall = 16 if rows % 16 == 0 else 8
    pairs = [(part, energy) for part in range(2) for energy in range(energies)]

    def chunk(number, carry):
        row = pl.multiple_of(number * tall, tall)
        place = (pl.ds(row, tall), pl.ds(begin, wide))
        target = [None] * kinds
        for part, energy in pairs:
            plane = data[(part, energy) + place]
            for kind in range(kinds):
                term = materials_ref[part, energy, kind] * plane
                target[kind] = term if target[kind] is None else target[kind] + term
        target = [rate * value for value in target]
        current = [jnp.maximum(value, 0.0) for value in target]

        def descend(turn, current):
            following = []
            for one in range(kinds):
                total = target[one]
                for other in range(kinds):
                    total = total + step_ref[one * kinds + other] * current[other]
                following.append(jnp.maximum(total, 0.0))
            return following

        current = lax.fori_loop(1, FIT_STEPS, descend, current)
        for part, energy in pairs:
            total = None
            for kind in range(kinds):
                term = materials_ref[part, energy, kind] * current[kind]
                total = term if total is None else total + term
            spectra[(part, energy) + place] = total
        return carry

    lax.fori_loop(0, rows // tall, chunk, 0)


def exchange_kernel(
    groups,
    tiles,
    fold,
    materials_ref,
    gradient,
    field,
    probe,
    out_ref,
    step_ref,
    main,
    side,
    margin,
    data,
    spectra,
    margin_sems,
    send_sems,
    recv_sems,
    own_sems,
):
    mesh_ids = pl.DeviceIdType.MESH
    me = lax.axis_index("energy")
    tile = lax.axis_index("tile")
    after = lax.rem(tile + 1, tiles)
    before = lax.rem(tile + tiles - 1, tiles)
    tile_px = out_ref.shape[-1]
    length = probe.shape[2]
    blocks = tile_px // LANES
    rows = tile_px // groups
    kinds = materials_ref.shape[2]
    offsets = sorted(range(1, groups), key=lambda offset: abs(offset - groups // 2))
    peers = {offset: lax.rem(me + offset, groups) for offset in offsets}

    barrier = pltpu.get_barrier_semaphore()
    pl.semaphore_signal(barrier, inc=1, device_id=(me, before), device_id_type=mesh_ids)
    for offset in offsets:
        pl.semaphore_signal(
            barrier, inc=1, device_id=(peers[offset], tile), device_id_type=mesh_ids
        )

    peak = jnp.max(probe[0] * probe[0] + probe[1] * probe[1])
    tall = 64
    inverse = 1.0 / jnp.full((tall, LANES), peak, jnp.float32)

    def finish(wrapped, number, carry):
        place = (pl.ds(pl.multiple_of(number * tall, tall), tall), slice(None))
        beyond = pl.ds(pl.multiple_of(tile_px + number * tall, tall), tall)
        for part in range(2):
            for block in range(field.shape[1]):
                value = gradient[(part, block) + place]
                if wrapped:
                    value = value + gradient[part, block, beyond, :]
                share = value * inverse
                if block < blocks:
                    main[(part, block) + place] = field[(part, block) + place] + share
                else:
                    side[(part, block - blocks) + place] = share
        return carry

    lax.fori_loop(0, length // tall, functools.partial(finish, fold), 0)
    lax.fori_loop(length // tall, tile_px // tall, functools.partial(finish, False), 0)

    pl.semaphore_wait(barrier, groups)

    margin_copy = pltpu.make_async_remote_copy(
        src_ref=side,
        dst_ref=margin,
        send_sem=margin_sems.at[0],
        recv_sem=margin_sems.at[1],
        device_id=(me, after),
        device_id_type=mesh_ids,
    )
    margin_copy.start()

    def rows_of(group):
        return pl.ds(pl.multiple_of(group * rows, rows), rows)

    def outward(block):
        columns = pl.ds(block * LANES, LANES)
        copies = [
            pltpu.make_async_remote_copy(
                src_ref=main.at[:, block, rows_of(peers[offset]), :],
                dst_ref=data.at[:, me, :, columns],
                send_sem=send_sems.at[0, block, offset],
                recv_sem=recv_sems.at[0, block, offset],
                device_id=(peers[offset], tile),
                device_id_type=mesh_ids,
            )
            for offset in offsets
        ]
        own = pltpu.make_async_copy(
            main.at[:, block, rows_of(me), :], data.at[:, me, :, columns], own_sems.at[0, block]
        )
        return copies, own

    def homeward(block):
        columns = pl.ds(block * LANES, LANES)
        copies = [
            pltpu.make_async_remote_copy(
                src_ref=spectra.at[:, peers[offset], :, columns],
                dst_ref=out_ref.at[:, rows_of(me), columns],
                send_sem=send_sems.at[1, block, offset],
                recv_sem=recv_sems.at[1, block, offset],
                device_id=(peers[offset], tile),
                device_id_type=mesh_ids,
            )
            for offset in offsets
        ]
        own = pltpu.make_async_copy(
            spectra.at[:, me, :, columns], out_ref.at[:, rows_of(me), columns], own_sems.at[1, block]
        )
        return copies, own

    def start(moves):
        for copy in moves[0]:
            copy.start()
        moves[1].start()

    early = [block for block in range(blocks) if block * LANES >= length]
    late = [block for block in range(blocks) if block * LANES < length]
    going = {}
    for block in early:
        going[block] = outward(block)
        start(going[block])

    gram, trace = fit_scalars(materials_ref, groups, kinds)
    rate = 1.0 / trace
    for one in range(kinds):
        for other in range(kinds):
            unit = 1.0 if one == other else 0.0
            step_ref[one * kinds + other] = unit - rate * gram[one][other]
    margin_copy.wait()
    for block in late:
        main[:, block] = main[:, block] + margin[:, block]
    for block in late:
        going[block] = outward(block)
        start(going[block])
    coming = {}
    for block in early + late:
        copies, own = going[block]
        for copy in copies:
            copy.wait_recv()
        own.wait()
        fit_columns(
            materials_ref, step_ref, data, spectra, groups, kinds, rate, block * LANES, LANES
        )
        coming[block] = homeward(block)
        start(coming[block])
    for block in early + late:
        for copy in going[block][0]:
            copy.wait_send()
        copies, own = coming[block]
        own.wait()
        for copy in copies:
            copy.wait()


def exchange_fit(gradient, field, probe, materials, fold):
    groups = lax.axis_size("energy")
    tiles = lax.axis_size("tile")
    pieces = probe.shape[1]
    blocks = field.shape[1] - pieces
    tile_px = blocks * LANES
    kinds = materials.shape[-1]
    rows = tile_px // groups
    vmem = pl.BlockSpec(memory_space=pltpu.VMEM)
    return pl.pallas_call(
        functools.partial(exchange_kernel, groups, tiles, fold),
        out_shape=jax.ShapeDtypeStruct((2, tile_px, tile_px), jnp.float32),
        in_specs=[pl.BlockSpec(memory_space=pltpu.SMEM), vmem, vmem, vmem],
        out_specs=vmem,
        scratch_shapes=[
            pltpu.SMEM((kinds * kinds,), jnp.float32),
            pltpu.VMEM((2, blocks, tile_px, LANES), jnp.float32),
            pltpu.VMEM((2, pieces, tile_px, LANES), jnp.float32),
            pltpu.VMEM((2, pieces, tile_px, LANES), jnp.float32),
            pltpu.VMEM((2, groups, rows, tile_px), jnp.float32),
            pltpu.VMEM((2, groups, rows, tile_px), jnp.float32),
            pltpu.SemaphoreType.DMA((2,)),
            pltpu.SemaphoreType.DMA((2, blocks, groups)),
            pltpu.SemaphoreType.DMA((2, blocks, groups)),
            pltpu.SemaphoreType.DMA((2, blocks)),
        ],
        compiler_params=pltpu.CompilerParams(
            collective_id=0, has_side_effects=True, vmem_limit_bytes=24 * 1024 * 1024
        ),
        name="exchange",
    )(materials, gradient, field, probe)


def body(object_tiles, probe_wave, measured, positions, materials):
    own_object = object_tiles[0, :, 0]
    tile_px = own_object.shape[-1]
    length = probe_wave.shape[-1]
    row_step = TILE_COLS % lax.axis_size("tile")
    fold = row_step == 0
    gradient, field, probe = patch_calls(
        own_object,
        probe_wave[0],
        measured[0, 0],
        positions[0].T,
        fold,
        functools.partial(shifted, axis="tile", steps=-1),
    )
    if not fold:
        from_above = shifted(gradient[:, :, tile_px:], "tile", row_step)
        gradient = gradient.at[:, :, :length].add(from_above)
    fitted = exchange_fit(gradient, field, probe, materials, fold)
    return fitted.reshape(1, 2, 1, tile_px, tile_px)


def solution(mesh):
    in_specs = (
        P("energy", None, "tile", None, None),
        P("energy", None, None, None),
        P("energy", "tile", None, None, None),
        P("tile", None, None),
        P(),
    )
    out_specs = P("energy", None, "tile", None, None)
    return jax.shard_map(body, mesh=mesh, in_specs=in_specs, out_specs=out_specs, check_vma=False)
```

```python
import functools
import math

import jax
import jax.numpy as jnp
import numpy as np
from jax import lax
from jax.experimental import pallas as pl
from jax.experimental.pallas import tpu as pltpu
from jax.sharding import PartitionSpec as P


TILE_COLS = 4
FIT_STEPS = 10
LANES = 128
VMEM_LIMIT = 12 * 1024 * 1024
LOAD_LIMIT = 8 * 1024 * 1024


amplitude_floor = 0.5


def shifted(value, axis, steps):
    count = lax.axis_size(axis)
    pairs = [(source, (source + steps) % count) for source in range(count)]
    return lax.ppermute(value, axis, pairs)


def trig_parts(rows, columns, length):
    angles = 2.0 * math.pi / length * (rows[:, None] * columns[None, :] % length)
    return np.stack([np.cos(angles), np.sin(angles)]).astype(np.float32).astype(jnp.bfloat16)


def fourier_parts(length):
    counter = np.arange(length, dtype=np.int64)
    half = counter[: length // 2]
    left = np.stack([trig_parts(half, counter[parity::2], length) for parity in range(2)])
    return jnp.asarray(left), jnp.asarray(trig_parts(counter, counter, length))


def joined(top_left, top_right, bottom_left, bottom_right):
    return jnp.concatenate(
        [
            jnp.concatenate([top_left, top_right], 1),
            jnp.concatenate([bottom_left, bottom_right], 1),
        ],
        0,
    )


def transform(even, odd, left_ref, right_ref):
    length = even.shape[0]
    half = length // 2
    one = jnp.dot(left_ref[0], even, preferred_element_type=jnp.float32)
    two = jnp.dot(left_ref[1], odd, preferred_element_type=jnp.float32)
    upper = (one + two).astype(jnp.bfloat16)
    lower = (one - two).astype(jnp.bfloat16)
    beside = joined(upper[:half], upper[half:], lower[:half], lower[half:])
    outer = jnp.dot(beside, right_ref[...], preferred_element_type=jnp.float32)
    return outer[:, :length], outer[:, length:]


def window(ref, part, rows, block, shift, length):
    lane = lax.broadcasted_iota(jnp.int32, (rows.size, LANES), 1)
    back = lax.rem(LANES - shift, LANES)
    tiles = [
        pltpu.roll(ref[part, block + at, rows, :], back, 1) for at in range(length // LANES + 1)
    ]
    keep = lane < LANES - shift
    return jnp.concatenate(
        [jnp.where(keep, one, other) for one, other in zip(tiles[:-1], tiles[1:])], 1
    )


def add_window(ref, part, row, block, shift, term):
    length = term.shape[0]
    lane = lax.broadcasted_iota(jnp.int32, (length, LANES), 1)
    tiles = [pltpu.roll(term[:, at : at + LANES], shift, 1) for at in range(0, length, LANES)]
    keep = lane >= shift
    zero = jnp.zeros_like(tiles[0])
    for at, (one, other) in enumerate(zip(tiles + [zero], [zero] + tiles)):
        place = (part, block + at, pl.ds(row, length), slice(None))
        ref[place] = ref[place] + jnp.where(keep, one, other)


def load_kernel(object_ref, probe_ref, left_ref, right_ref, *refs):
    *strips, early, late, gradient, terms, left, right, probe, split = refs[:-4]
    edge, parts_left, parts_right, sems = refs[-4:]
    length = probe_ref.shape[-1]
    half = length // 2
    pieces = length // LANES
    moves = [(left_ref, parts_left), (right_ref, parts_right)]
    for piece, strip in enumerate([*strips, edge]):
        moves.append((object_ref.at[:, :, pl.ds(piece * LANES, LANES)], strip))
    for piece in range(pieces):
        columns = pl.ds(piece * LANES, LANES)
        moves.append((probe_ref.at[:, :, columns], probe.at[:, piece]))
    copies = [
        pltpu.make_async_copy(source, target, sems.at[number])
        for number, (source, target) in enumerate(moves)
    ]
    for copy in copies:
        copy.start()
    gradient[...] = jnp.zeros_like(gradient)
    terms[...] = jnp.zeros_like(terms)
    for copy in copies[:2]:
        copy.wait()
    for parity in range(2):
        cosine = parts_left[parity, 0]
        sine = parts_left[parity, 1]
        left[0, parity] = joined(cosine, sine, -sine, cosine)
        left[1, parity] = joined(cosine, -sine, sine, cosine)
    scale = jnp.asarray(1.0 / length, jnp.bfloat16)
    cosine = parts_right[0] * scale
    sine = parts_right[1] * scale
    right[0] = joined(cosine, -sine, sine, cosine)
    right[1] = joined(cosine, sine, -sine, cosine)
    for copy in copies[2:]:
        copy.wait()
    middle = edge.shape[1] // 2
    low = lax.broadcasted_iota(jnp.int32, (middle, LANES), 1) < LANES // 2
    for part in range(2):
        upper = edge[part, :middle]
        lower = edge[part, middle:]
        early[part] = jnp.where(low, upper, pltpu.roll(lower, LANES // 2, 1))
        late[part] = jnp.where(low, pltpu.roll(upper, LANES // 2, 1), lower)
    for parity in range(2):
        for part in range(2):
            for piece in range(pieces):
                columns = slice(piece * LANES, (piece + 1) * LANES)
                rows = pl.ds(parity, half, stride=2)
                split[parity, part, :, columns] = probe[part, piece, rows, :]


def patch_kernel(fold, phase, phases, *refs):
    first = phase == 0
    last = phase == phases - 1
    lower_count = 1 if last and not fold else 0
    lead = 2 + lower_count
    corners_ref = refs[0]
    source_ref = refs[1]
    lower_ref = refs[2] if lower_count else None
    held, left, right, probe, split = refs[lead : lead + 5]
    refs = refs[lead + 5 + (2 if first else 5) :]
    gradient, terms, field, wave, change = refs[:5]
    order, sems = refs[-2:]
    length = wave.shape[-1]
    half = length // 2
    pieces = length // LANES
    width = field.shape[1]
    blocks = width - pieces
    tile_px = blocks * LANES
    count = held.shape[0]
    limit = tile_px - length
    top = pl.ds(0, tile_px)
    bottom = pl.ds(tile_px, length)
    moves = []
    if first:
        for block in range(blocks):
            columns = pl.ds(block * LANES, LANES)
            moves.append((source_ref.at[:, :, columns], field.at[:, block, top, :]))
            if fold:
                source = source_ref.at[:, pl.ds(0, length), columns]
                moves.append((source, field.at[:, block, bottom, :]))
    elif phase < pieces:
        block = blocks + phase - 1
        moves.append((source_ref, field.at[:, block, top, :]))
        if fold:
            source = source_ref.at[:, pl.ds(0, length), :]
            moves.append((source, field.at[:, block, bottom, :]))
    if last and not fold:
        for block in range(width):
            columns = pl.ds(block * LANES, LANES)
            moves.append((lower_ref.at[:, :, columns], field.at[:, block, bottom, :]))
    copies = [
        pltpu.make_async_copy(source, target, sems.at[number])
        for number, (source, target) in enumerate(moves)
    ]
    for copy in copies:
        copy.start()

    bounds = [LANES * piece for piece in range(pieces)] + [length - LANES // 2]

    def rank(number):
        beyond = corners_ref[1, number] - limit
        kind = sum(jnp.where(beyond > bound, 8, 0) for bound in bounds)
        if not fold:
            kind = jnp.where(corners_ref[0, number] > limit, 8 * (phases - 1), kind)
        return kind

    kinds = [rank(number) for number in range(count)]
    total = sum(jnp.left_shift(1, kind) for kind in kinds)
    place = sum(jnp.left_shift(total, 8 * step) for step in range(1, phases))
    ends = [
        lax.bitwise_and(jnp.right_shift(total + place, 8 * step), 255) for step in range(phases)
    ]
    for number, kind in enumerate(kinds):
        order[lax.bitwise_and(jnp.right_shift(place, kind), 255)] = number
        place = place + jnp.left_shift(1, kind)
    if phase >= pieces:
        middle = tile_px // 2
        low = lax.broadcasted_iota(jnp.int32, (middle, LANES), 1) < LANES // 2
        for part in range(2):
            packed = source_ref[part]
            rolled = pltpu.roll(packed, LANES // 2, 1)
            if last:
                upper = jnp.where(low, field[part, width - 1, :middle], rolled)
                lower = jnp.where(low, field[part, width - 1, middle:tile_px], packed)
            else:
                upper, lower = packed, rolled
            field[part, width - 1, :middle] = upper
            field[part, width - 1, middle:tile_px] = lower
            if fold:
                field[part, width - 1, tile_px:] = jnp.concatenate([upper, lower], 0)[:length]
    begin = jnp.maximum(ends[phase - 1] - 2, 0) if phase else 0
    end = count - 1 if last else jnp.maximum(ends[phase] - 2, 0)
    for copy in copies:
        copy.wait()

    def corner(turn):
        number = order[turn]
        row = corners_ref[0, number]
        col = corners_ref[1, number]
        block = col // LANES
        return number, row, block, col - block * LANES

    def gather(turn):
        _, row, block, shift = corner(turn)
        for parity in range(2):
            rows = pl.ds(row + parity, half, stride=2)
            piece_real = window(field, 0, rows, block, shift, length)
            piece_imag = window(field, 1, rows, block, shift, length)
            probe_real = split[parity, 0]
            probe_imag = split[parity, 1]
            exit_real = probe_real * piece_real - probe_imag * piece_imag
            exit_imag = probe_real * piece_imag + probe_imag * piece_real
            wave[parity, :half, :] = exit_real.astype(jnp.bfloat16)
            wave[parity, half:, :] = exit_imag.astype(jnp.bfloat16)

    def scatter(turn):
        _, row, block, shift = corner(turn)
        add_window(gradient, 0, row, block, shift, terms[0])
        add_window(gradient, 1, row, block, shift, terms[1])

    def outward(turn):
        far_real, far_imag = transform(wave[0], wave[1], left.at[0], right.at[0])
        square = far_real * far_real + far_imag * far_imag
        scale = lax.rsqrt(jnp.maximum(square, amplitude_floor * amplitude_floor))
        factor = held[order[turn]].astype(jnp.float32) * scale - 1.0
        return factor * far_real, factor * far_imag

    def keep(parts):
        for part in range(2):
            for piece in range(pieces):
                change[part, piece] = parts[part][:, piece * LANES : (piece + 1) * LANES]

    def changed(parity):
        rows = pl.ds(parity, half, stride=2)
        return jnp.concatenate(
            [
                jnp.concatenate([change[part, piece, rows, :] for piece in range(pieces)], 1)
                for part in range(2)
            ],
            0,
        ).astype(jnp.bfloat16)

    def homeward():
        back_real, back_imag = transform(changed(0), changed(1), left.at[1], right.at[1])
        probe_real = jnp.concatenate([probe[0, piece] for piece in range(pieces)], 1)
        probe_imag = jnp.concatenate([probe[1, piece] for piece in range(pieces)], 1)
        return (
            probe_real * back_real + probe_imag * back_imag,
            probe_real * back_imag - probe_imag * back_real,
        )

    def step(turn, carry):
        scatter(jnp.maximum(turn - 1, 0))
        parts = outward(turn + 1)
        back = homeward()
        keep(parts)
        gather(jnp.minimum(turn + 2, count - 1))
        terms[0] = back[0]
        terms[1] = back[1]
        return carry

    ready = ends[phase] >= 2
    if not first:
        ready = jnp.logical_and(ready, ends[phase - 1] < 2)

    @pl.when(ready)
    def _():
        gather(0)
        keep(outward(0))
        gather(1)

    lax.fori_loop(begin, end, step, 0)
    if last:
        scatter(count - 2)
        back = homeward()
        terms[0] = back[0]
        terms[1] = back[1]
        scatter(count - 1)


def patch_calls(own_object, probe, measured, corners, fold, shift):
    tile_px = own_object.shape[-1]
    length = probe.shape[-1]
    count = measured.shape[0]
    width = tile_px + length
    pieces = length // LANES
    phases = 2 + pieces
    vmem = pl.BlockSpec(memory_space=pltpu.VMEM)
    anywhere = pl.BlockSpec(memory_space=pl.ANY)
    smem = pl.BlockSpec(memory_space=pltpu.SMEM)

    def single(*shape):
        return jax.ShapeDtypeStruct(shape, jnp.float32)

    def brief(*shape):
        return jax.ShapeDtypeStruct(shape, jnp.bfloat16)

    sums = (2, width // LANES, width, LANES)
    moving = [
        single(*sums),
        single(2, length, length),
        single(*sums),
        brief(2, length, length),
        single(2, pieces, length, LANES),
    ]
    fixed = [
        brief(2, 2, length, length),
        brief(2, 2 * length, 2 * length),
        single(2, pieces, length, LANES),
        single(2, 2, length // 2, length),
    ]
    strips = [single(2, tile_px, LANES)] * (pieces - 1) + [single(2, tile_px // 2, LANES)] * 2
    loaded = strips + moving[:2] + fixed
    parts_left, parts_right = fourier_parts(length)
    sources = (own_object, probe, parts_left, parts_right)
    out = pl.pallas_call(
        load_kernel,
        out_shape=loaded,
        in_specs=[anywhere] * 4,
        out_specs=[vmem] * len(loaded),
        scratch_shapes=[
            pltpu.VMEM((2, tile_px, LANES), jnp.float32),
            pltpu.VMEM(parts_left.shape, jnp.bfloat16),
            pltpu.VMEM(parts_right.shape, jnp.bfloat16),
            pltpu.SemaphoreType.DMA((2 + 2 * pieces,)),
        ],
        compiler_params=pltpu.CompilerParams(vmem_limit_bytes=LOAD_LIMIT),
        cost_estimate=pl.CostEstimate(flops=10**10, bytes_accessed=2**24, transcendentals=0),
        name="load",
    )(*(pltpu.with_memory_space_constraint(value, pltpu.HBM) for value in sources))
    strips = []
    for strip in out[: pieces + 1]:
        strips.append(shift(strip))
    state = list(out[pieces + 1 : pieces + 3])
    held = [measured, *out[pieces + 3 :]]
    for phase in range(phases):
        last = phase == phases - 1
        more = [strips[phase - 1] if phase else own_object]
        if last and not fold:
            wide = [strip[:, :length] for strip in strips[:-2]]
            wide += [strip[:, :length, : LANES // 2] for strip in strips[-2:]]
            widened = jnp.concatenate([own_object[:, :length]] + wide, 2)
            more.append(shifted(widened, "tile", -(TILE_COLS % lax.axis_size("tile"))))
        lead = 1 + len(more) + len(held)
        state = pl.pallas_call(
            functools.partial(patch_kernel, fold, phase, phases),
            out_shape=moving,
            in_specs=[smem]
            + [vmem if phase >= pieces else anywhere]
            + [anywhere] * (len(more) - 1)
            + [vmem] * (len(held) + len(state)),
            out_specs=[vmem] * len(moving),
            scratch_shapes=[
                pltpu.SMEM((count,), jnp.int32),
                pltpu.SemaphoreType.DMA((2 * (width // LANES),)),
            ],
            input_output_aliases={lead + at: at for at in range(len(state))},
            compiler_params=pltpu.CompilerParams(vmem_limit_bytes=VMEM_LIMIT),
            cost_estimate=pl.CostEstimate(
                flops=8 * count * length**3,
                bytes_accessed=8 * tile_px * tile_px,
                transcendentals=0,
            ),
        )(corners, *more, *held, *state)
    return state[0], state[2], held[3]


def fit_scalars(materials_ref, energies, kinds):
    spectra = [
        [materials_ref[part, energy, kind] for kind in range(kinds)]
        for part in range(2)
        for energy in range(energies)
    ]
    gram = [[None] * kinds for _ in range(kinds)]
    for one in range(kinds):
        for other in range(one, kinds):
            total = spectra[0][one] * spectra[0][other]
            for row in spectra[1:]:
                total = total + row[one] * row[other]
            gram[one][other] = total
            gram[other][one] = total
    trace = gram[0][0]
    for one in range(1, kinds):
        trace = trace + gram[one][one]
    return gram, trace


def fit_columns(materials_ref, step_ref, data, spectra, energies, kinds, rate, begin, wide):
    rows = data.shape[2]
    tall = 16 if rows % 16 == 0 else 8
    pairs = [(part, energy) for part in range(2) for energy in range(energies)]

    def chunk(number, carry):
        row = pl.multiple_of(number * tall, tall)
        place = (pl.ds(row, tall), pl.ds(begin, wide))
        target = [None] * kinds
        for part, energy in pairs:
            plane = data[(part, energy) + place]
            for kind in range(kinds):
                term = materials_ref[part, energy, kind] * plane
                target[kind] = term if target[kind] is None else target[kind] + term
        target = [rate * value for value in target]
        current = [jnp.maximum(value, 0.0) for value in target]

        def descend(turn, current):
            following = []
            for one in range(kinds):
                total = target[one]
                for other in range(kinds):
                    total = total + step_ref[one * kinds + other] * current[other]
                following.append(jnp.maximum(total, 0.0))
            return following

        current = lax.fori_loop(1, FIT_STEPS, descend, current)
        for part, energy in pairs:
            total = None
            for kind in range(kinds):
                term = materials_ref[part, energy, kind] * current[kind]
                total = term if total is None else total + term
            spectra[(part, energy) + place] = total
        return carry

    lax.fori_loop(0, rows // tall, chunk, 0)


def exchange_kernel(
    groups,
    tiles,
    fold,
    materials_ref,
    gradient,
    field,
    probe,
    out_ref,
    step_ref,
    main,
    side,
    margin,
    data,
    spectra,
    margin_sems,
    send_sems,
    recv_sems,
    own_sems,
):
    mesh_ids = pl.DeviceIdType.MESH
    me = lax.axis_index("energy")
    tile = lax.axis_index("tile")
    after = lax.rem(tile + 1, tiles)
    before = lax.rem(tile + tiles - 1, tiles)
    tile_px = out_ref.shape[-1]
    length = probe.shape[2]
    blocks = tile_px // LANES
    rows = tile_px // groups
    kinds = materials_ref.shape[2]
    offsets = sorted(range(1, groups), key=lambda offset: abs(offset - groups // 2))
    peers = {offset: lax.rem(me + offset, groups) for offset in offsets}

    barrier = pltpu.get_barrier_semaphore()
    pl.semaphore_signal(barrier, inc=1, device_id=(me, before), device_id_type=mesh_ids)
    for offset in offsets:
        pl.semaphore_signal(
            barrier, inc=1, device_id=(peers[offset], tile), device_id_type=mesh_ids
        )

    peak = jnp.max(probe[0] * probe[0] + probe[1] * probe[1])
    tall = 64
    inverse = 1.0 / jnp.full((tall, LANES), peak, jnp.float32)

    early = [block for block in range(blocks) if block * LANES >= length]
    late = [block for block in range(blocks) if block * LANES < length]
    beyond_tile = list(range(blocks, field.shape[1]))

    def finish_rows(which, wrapped, number, carry):
        place = (pl.ds(pl.multiple_of(number * tall, tall), tall), slice(None))
        beyond = pl.ds(pl.multiple_of(tile_px + number * tall, tall), tall)
        for part in range(2):
            for block in which:
                value = gradient[(part, block) + place]
                if wrapped:
                    value = value + gradient[part, block, beyond, :]
                share = value * inverse
                if block < blocks:
                    main[(part, block) + place] = field[(part, block) + place] + share
                else:
                    side[(part, block - blocks) + place] = share
        return carry

    def finish(which):
        lax.fori_loop(0, length // tall, functools.partial(finish_rows, which, fold), 0)
        lax.fori_loop(
            length // tall, tile_px // tall, functools.partial(finish_rows, which, False), 0
        )

    finish(beyond_tile + early)
    pl.semaphore_wait(barrier, groups)

    margin_copy = pltpu.make_async_remote_copy(
        src_ref=side,
        dst_ref=margin,
        send_sem=margin_sems.at[0],
        recv_sem=margin_sems.at[1],
        device_id=(me, after),
        device_id_type=mesh_ids,
    )
    margin_copy.start()

    def rows_of(group):
        return pl.ds(pl.multiple_of(group * rows, rows), rows)

    def outward(block):
        columns = pl.ds(block * LANES, LANES)
        copies = [
            pltpu.make_async_remote_copy(
                src_ref=main.at[:, block, rows_of(peers[offset]), :],
                dst_ref=data.at[:, me, :, columns],
                send_sem=send_sems.at[0, block, offset],
                recv_sem=recv_sems.at[0, block, offset],
                device_id=(peers[offset], tile),
                device_id_type=mesh_ids,
            )
            for offset in offsets
        ]
        own = pltpu.make_async_copy(
            main.at[:, block, rows_of(me), :], data.at[:, me, :, columns], own_sems.at[0, block]
        )
        return copies, own

    def homeward(block):
        columns = pl.ds(block * LANES, LANES)
        copies = [
            pltpu.make_async_remote_copy(
                src_ref=spectra.at[:, peers[offset], :, columns],
                dst_ref=out_ref.at[:, rows_of(me), columns],
                send_sem=send_sems.at[1, block, offset],
                recv_sem=recv_sems.at[1, block, offset],
                device_id=(peers[offset], tile),
                device_id_type=mesh_ids,
            )
            for offset in offsets
        ]
        own = pltpu.make_async_copy(
            spectra.at[:, me, :, columns], out_ref.at[:, rows_of(me), columns], own_sems.at[1, block]
        )
        return copies, own

    def start(moves):
        for copy in moves[0]:
            copy.start()
        moves[1].start()

    going = {}
    for block in early:
        going[block] = outward(block)
        start(going[block])
    finish(late)

    gram, trace = fit_scalars(materials_ref, groups, kinds)
    rate = 1.0 / trace
    for one in range(kinds):
        for other in range(kinds):
            unit = 1.0 if one == other else 0.0
            step_ref[one * kinds + other] = unit - rate * gram[one][other]
    margin_copy.wait()
    for block in late:
        main[:, block] = main[:, block] + margin[:, block]
    for block in late:
        going[block] = outward(block)
        start(going[block])
    coming = {}
    for block in early + late:
        copies, own = going[block]
        for copy in copies:
            copy.wait_recv()
        own.wait()
        fit_columns(
            materials_ref, step_ref, data, spectra, groups, kinds, rate, block * LANES, LANES
        )
        coming[block] = homeward(block)
        start(coming[block])
    for block in early + late:
        for copy in going[block][0]:
            copy.wait_send()
        copies, own = coming[block]
        own.wait()
        for copy in copies:
            copy.wait()


def exchange_fit(gradient, field, probe, materials, fold):
    groups = lax.axis_size("energy")
    tiles = lax.axis_size("tile")
    pieces = probe.shape[1]
    blocks = field.shape[1] - pieces
    tile_px = blocks * LANES
    kinds = materials.shape[-1]
    rows = tile_px // groups
    vmem = pl.BlockSpec(memory_space=pltpu.VMEM)
    return pl.pallas_call(
        functools.partial(exchange_kernel, groups, tiles, fold),
        out_shape=jax.ShapeDtypeStruct((2, tile_px, tile_px), jnp.float32),
        in_specs=[pl.BlockSpec(memory_space=pltpu.SMEM), vmem, vmem, vmem],
        out_specs=vmem,
        scratch_shapes=[
            pltpu.SMEM((kinds * kinds,), jnp.float32),
            pltpu.VMEM((2, blocks, tile_px, LANES), jnp.float32),
            pltpu.VMEM((2, pieces, tile_px, LANES), jnp.float32),
            pltpu.VMEM((2, pieces, tile_px, LANES), jnp.float32),
            pltpu.VMEM((2, groups, rows, tile_px), jnp.float32),
            pltpu.VMEM((2, groups, rows, tile_px), jnp.float32),
            pltpu.SemaphoreType.DMA((2,)),
            pltpu.SemaphoreType.DMA((2, blocks, groups)),
            pltpu.SemaphoreType.DMA((2, blocks, groups)),
            pltpu.SemaphoreType.DMA((2, blocks)),
        ],
        compiler_params=pltpu.CompilerParams(
            collective_id=0, has_side_effects=True, vmem_limit_bytes=24 * 1024 * 1024
        ),
        name="exchange",
    )(materials, gradient, field, probe)


def body(object_tiles, probe_wave, measured, positions, materials):
    own_object = object_tiles[0, :, 0]
    tile_px = own_object.shape[-1]
    length = probe_wave.shape[-1]
    row_step = TILE_COLS % lax.axis_size("tile")
    fold = row_step == 0
    gradient, field, probe = patch_calls(
        own_object,
        probe_wave[0],
        measured[0, 0],
        positions[0].T,
        fold,
        functools.partial(shifted, axis="tile", steps=-1),
    )
    if not fold:
        from_above = shifted(gradient[:, :, tile_px:], "tile", row_step)
        gradient = gradient.at[:, :, :length].add(from_above)
    fitted = exchange_fit(gradient, field, probe, materials, fold)
    return fitted.reshape(1, 2, 1, tile_px, tile_px)


def solution(mesh):
    in_specs = (
        P("energy", None, "tile", None, None),
        P("energy", None, None, None),
        P("energy", "tile", None, None, None),
        P("tile", None, None),
        P(),
    )
    out_specs = P("energy", None, "tile", None, None)

    return jax.shard_map(body, mesh=mesh, in_specs=in_specs, out_specs=out_specs, check_vma=False)
```

```python
import functools
import math

import jax
import jax.numpy as jnp
import numpy as np
from jax import lax
from jax.experimental import pallas as pl
from jax.experimental.pallas import tpu as pltpu
from jax.sharding import PartitionSpec as P

TILE_COLS = 4
FIT_STEPS = 10
LANES = 128
LATE = 8
VMEM_LIMIT = 12 * 1024 * 1024
LOAD_LIMIT = 8 * 1024 * 1024


amplitude_floor = 0.5


def shifted(value, axis, steps):
    count = lax.axis_size(axis)
    pairs = [(source, (source + steps) % count) for source in range(count)]
    return lax.ppermute(value, axis, pairs)


def trig_parts(rows, columns, length):
    angles = 2.0 * math.pi / length * (rows[:, None] * columns[None, :] % length)
    return np.stack([np.cos(angles), np.sin(angles)]).astype(np.float32).astype(jnp.bfloat16)


def fourier_parts(length):
    counter = np.arange(length, dtype=np.int64)
    half = counter[: length // 2]
    left = np.stack([trig_parts(half, counter[parity::2], length) for parity in range(2)])
    return jnp.asarray(left), jnp.asarray(trig_parts(counter, counter, length))


def joined(top_left, top_right, bottom_left, bottom_right):
    return jnp.concatenate(
        [
            jnp.concatenate([top_left, top_right], 1),
            jnp.concatenate([bottom_left, bottom_right], 1),
        ],
        0,
    )


def transform(even, odd, left_ref, right_ref):
    length = even.shape[0]
    half = length // 2
    one = jnp.dot(left_ref[0], even, preferred_element_type=jnp.float32)
    two = jnp.dot(left_ref[1], odd, preferred_element_type=jnp.float32)
    upper = (one + two).astype(jnp.bfloat16)
    lower = (one - two).astype(jnp.bfloat16)
    beside = joined(upper[:half], upper[half:], lower[:half], lower[half:])
    outer = jnp.dot(beside, right_ref[...], preferred_element_type=jnp.float32)
    return outer[:, :length], outer[:, length:]


def window(ref, part, rows, block, shift, length):
    lane = lax.broadcasted_iota(jnp.int32, (rows.size, LANES), 1)
    back = lax.rem(LANES - shift, LANES)
    tiles = [
        pltpu.roll(ref[part, block + at, rows, :], back, 1) for at in range(length // LANES + 1)
    ]
    keep = lane < LANES - shift
    return jnp.concatenate(
        [jnp.where(keep, one, other) for one, other in zip(tiles[:-1], tiles[1:])], 1
    )


def add_window(ref, part, row, block, shift, term):
    length = term.shape[0]
    lane = lax.broadcasted_iota(jnp.int32, (length, LANES), 1)
    tiles = [pltpu.roll(term[:, at : at + LANES], shift, 1) for at in range(0, length, LANES)]
    keep = lane >= shift
    zero = jnp.zeros_like(tiles[0])
    for at, (one, other) in enumerate(zip(tiles + [zero], [zero] + tiles)):
        place = (part, block + at, pl.ds(row, length), slice(None))
        ref[place] = ref[place] + jnp.where(keep, one, other)


def load_kernel(object_ref, probe_ref, left_ref, right_ref, *refs):
    *strips, gradient, terms, left, right, probe, split = refs[:-3]
    parts_left, parts_right, sems = refs[-3:]
    length = probe_ref.shape[-1]
    half = length // 2
    pieces = length // LANES
    moves = [(left_ref, parts_left), (right_ref, parts_right)]
    for piece, strip in enumerate(strips):
        moves.append((object_ref.at[:, :, pl.ds(piece * LANES, LANES)], strip))
    for piece in range(pieces):
        columns = pl.ds(piece * LANES, LANES)
        moves.append((probe_ref.at[:, :, columns], probe.at[:, piece]))
    copies = [
        pltpu.make_async_copy(source, target, sems.at[number])
        for number, (source, target) in enumerate(moves)
    ]
    for copy in copies:
        copy.start()
    gradient[...] = jnp.zeros_like(gradient)
    terms[...] = jnp.zeros_like(terms)
    for copy in copies[:2]:
        copy.wait()
    for parity in range(2):
        cosine = parts_left[parity, 0]
        sine = parts_left[parity, 1]
        left[0, parity] = joined(cosine, sine, -sine, cosine)
        left[1, parity] = joined(cosine, -sine, sine, cosine)
    scale = jnp.asarray(1.0 / length, jnp.bfloat16)
    cosine = parts_right[0] * scale
    sine = parts_right[1] * scale
    right[0] = joined(cosine, -sine, sine, cosine)
    right[1] = joined(cosine, sine, -sine, cosine)
    for copy in copies[2:]:
        copy.wait()
    for parity in range(2):
        for part in range(2):
            for piece in range(pieces):
                columns = slice(piece * LANES, (piece + 1) * LANES)
                rows = pl.ds(parity, half, stride=2)
                split[parity, part, :, columns] = probe[part, piece, rows, :]


def patch_stages(corners_ref, order, field, held, left, right, probe, split, wave, change):
    length = wave.shape[-1]
    half = length // 2
    pieces = length // LANES

    def corner(turn):
        number = order[turn]
        row = corners_ref[0, number]
        col = corners_ref[1, number]
        block = col // LANES
        return number, row, block, col - block * LANES

    def gather(turn):
        _, row, block, shift = corner(turn)
        for parity in range(2):
            rows = pl.ds(row + parity, half, stride=2)
            piece_real = window(field, 0, rows, block, shift, length)
            piece_imag = window(field, 1, rows, block, shift, length)
            probe_real = split[parity, 0]
            probe_imag = split[parity, 1]
            exit_real = probe_real * piece_real - probe_imag * piece_imag
            exit_imag = probe_real * piece_imag + probe_imag * piece_real
            wave[parity, :half, :] = exit_real.astype(jnp.bfloat16)
            wave[parity, half:, :] = exit_imag.astype(jnp.bfloat16)

    def outward(turn):
        far_real, far_imag = transform(wave[0], wave[1], left.at[0], right.at[0])
        square = far_real * far_real + far_imag * far_imag
        scale = lax.rsqrt(jnp.maximum(square, amplitude_floor * amplitude_floor))
        factor = held[order[turn]].astype(jnp.float32) * scale - 1.0
        return factor * far_real, factor * far_imag

    def keep(parts):
        for part in range(2):
            for piece in range(pieces):
                change[part, piece] = parts[part][:, piece * LANES : (piece + 1) * LANES]

    def changed(parity):
        rows = pl.ds(parity, half, stride=2)
        return jnp.concatenate(
            [
                jnp.concatenate([change[part, piece, rows, :] for piece in range(pieces)], 1)
                for part in range(2)
            ],
            0,
        ).astype(jnp.bfloat16)

    def homeward():
        back_real, back_imag = transform(changed(0), changed(1), left.at[1], right.at[1])
        probe_real = jnp.concatenate([probe[0, piece] for piece in range(pieces)], 1)
        probe_imag = jnp.concatenate([probe[1, piece] for piece in range(pieces)], 1)
        return (
            probe_real * back_real + probe_imag * back_imag,
            probe_real * back_imag - probe_imag * back_real,
        )

    return corner, gather, outward, keep, homeward


def patch_order(corners_ref, count, phases, limit, fold):
    def rank(number):
        beyond = corners_ref[1, number] - limit
        kind = sum(jnp.where(beyond > step * LANES, 8, 0) for step in range(phases - 1))
        if not fold:
            kind = jnp.where(corners_ref[0, number] > limit, 8 * (phases - 1), kind)
        return kind

    kinds = [rank(number) for number in range(count)]
    total = sum(jnp.left_shift(1, kind) for kind in kinds)
    place = sum(jnp.left_shift(total, 8 * step) for step in range(1, phases))
    ends = [
        lax.bitwise_and(jnp.right_shift(total + place, 8 * step), 255) for step in range(phases)
    ]
    spots = []
    for kind in kinds:
        spots.append(lax.bitwise_and(jnp.right_shift(place, kind), 255))
        place = place + jnp.left_shift(1, kind)
    return spots, ends


def late_count(count, fold):
    return min(LATE, count) if fold else 0


def patch_kernel(fold, phase, phases, *refs):
    first = phase == 0
    last = phase == phases - 1
    lower_count = 1 if last and not fold else 0
    lead = 2 + lower_count
    corners_ref = refs[0]
    source_ref = refs[1]
    lower_ref = refs[2] if lower_count else None
    held, left, right, probe, split = refs[lead : lead + 5]
    refs = refs[lead + 5 + (2 if first else 5) :]
    gradient, terms, field, wave, change = refs[:5]
    order, sems = refs[-2:]
    length = wave.shape[-1]
    half = length // 2
    pieces = length // LANES
    width = field.shape[1]
    blocks = width - pieces
    tile_px = blocks * LANES
    count = held.shape[0]
    limit = tile_px - length
    top = pl.ds(0, tile_px)
    bottom = pl.ds(tile_px, length)
    moves = []
    if first:
        for block in range(blocks):
            columns = pl.ds(block * LANES, LANES)
            moves.append((source_ref.at[:, :, columns], field.at[:, block, top, :]))
            if fold:
                source = source_ref.at[:, pl.ds(0, length), columns]
                moves.append((source, field.at[:, block, bottom, :]))
    else:
        block = blocks + phase - 1
        moves.append((source_ref, field.at[:, block, top, :]))
        if fold:
            moves.append((source_ref.at[:, pl.ds(0, length), :], field.at[:, block, bottom, :]))
        elif last:
            for block in range(width):
                columns = pl.ds(block * LANES, LANES)
                moves.append((lower_ref.at[:, :, columns], field.at[:, block, bottom, :]))
    copies = [
        pltpu.make_async_copy(source, target, sems.at[number])
        for number, (source, target) in enumerate(moves)
    ]
    for copy in copies:
        copy.start()

    spots, ends = patch_order(corners_ref, count, phases, limit, fold)
    for number, spot in enumerate(spots):
        order[spot] = number
    for copy in copies:
        copy.wait()
    corner, gather, outward, keep, homeward = patch_stages(
        corners_ref, order, field, held, left, right, probe, split, wave, change
    )

    def scatter(turn):
        _, row, block, shift = corner(turn)
        add_window(gradient, 0, row, block, shift, terms[0])
        add_window(gradient, 1, row, block, shift, terms[1])

    def leave(turn):
        back = homeward()
        terms[0] = back[0]
        terms[1] = back[1]

    def step(low, high, turn, carry):
        scatter(jnp.maximum(turn - 1, low))
        parts = outward(turn + 1)
        back = homeward()
        keep(parts)
        gather(jnp.minimum(turn + 2, high - 1))
        terms[0] = back[0]
        terms[1] = back[1]
        return carry

    def enter(low, high):
        gather(low)
        keep(outward(low))
        gather(jnp.minimum(low + 1, high - 1))

    def drain(low, high):
        scatter(jnp.maximum(high - 2, low))
        leave(high - 1)
        scatter(high - 1)

    if last:
        low = ends[phases - 2]
        high = jnp.maximum(low, count - late_count(count, fold))

        @pl.when(high > low)
        def _():
            terms[...] = jnp.zeros_like(terms)
            enter(low, high)
            lax.fori_loop(low, high - 1, functools.partial(step, low, high), 0)
            drain(low, high)

        return
    draining = phase == phases - 2
    high = ends[phase]
    before = ends[phase - 1] if phase else 0
    enough = 1 if draining else 2

    @pl.when(jnp.logical_and(high >= enough, before < 2))
    def _():
        enter(0, high)

    begin = jnp.maximum(before - 2, 0)
    end = high - 1 if draining else jnp.maximum(high - 2, 0)
    lax.fori_loop(begin, end, functools.partial(step, 0, high), 0)
    if draining:

        @pl.when(high > 0)
        def _():
            drain(0, high)


def patch_calls(own_object, probe, measured, corners, fold, shift):
    tile_px = own_object.shape[-1]
    length = probe.shape[-1]
    count = measured.shape[0]
    width = tile_px + length
    pieces = length // LANES
    phases = 1 + pieces
    vmem = pl.BlockSpec(memory_space=pltpu.VMEM)
    anywhere = pl.BlockSpec(memory_space=pl.ANY)
    smem = pl.BlockSpec(memory_space=pltpu.SMEM)

    def single(*shape):
        return jax.ShapeDtypeStruct(shape, jnp.float32)

    def brief(*shape):
        return jax.ShapeDtypeStruct(shape, jnp.bfloat16)

    sums = (2, width // LANES, width, LANES)
    moving = [
        single(*sums),
        single(2, length, length),
        single(*sums),
        brief(2, length, length),
        single(2, pieces, length, LANES),
    ]
    fixed = [
        brief(2, 2, length, length),
        brief(2, 2 * length, 2 * length),
        single(2, pieces, length, LANES),
        single(2, 2, length // 2, length),
    ]
    loaded = [single(2, tile_px, LANES)] * pieces + moving[:2] + fixed
    parts_left, parts_right = fourier_parts(length)
    sources = (own_object, probe, parts_left, parts_right)
    out = pl.pallas_call(
        load_kernel,
        out_shape=loaded,
        in_specs=[anywhere] * 4,
        out_specs=[vmem] * len(loaded),
        scratch_shapes=[
            pltpu.VMEM(parts_left.shape, jnp.bfloat16),
            pltpu.VMEM(parts_right.shape, jnp.bfloat16),
            pltpu.SemaphoreType.DMA((2 + 2 * pieces,)),
        ],
        compiler_params=pltpu.CompilerParams(vmem_limit_bytes=LOAD_LIMIT),
        cost_estimate=pl.CostEstimate(flops=10**10, bytes_accessed=2**24, transcendentals=0),
        name="load",
    )(*(pltpu.with_memory_space_constraint(value, pltpu.HBM) for value in sources))
    strips = [shift(strip) for strip in out[:pieces]]
    state = list(out[pieces : pieces + 2])
    held = [measured, *out[pieces + 2 :]]
    for phase in range(phases):
        last = phase == phases - 1
        more = [strips[phase - 1] if phase else own_object]
        if last and not fold:
            widened = jnp.concatenate(
                [own_object[:, :length]] + [strip[:, :length] for strip in strips], 2
            )
            more.append(shifted(widened, "tile", -(TILE_COLS % lax.axis_size("tile"))))
        lead = 1 + len(more) + len(held)
        state = pl.pallas_call(
            functools.partial(patch_kernel, fold, phase, phases),
            out_shape=moving,
            in_specs=[smem] + [anywhere] * len(more) + [vmem] * (len(held) + len(state)),
            out_specs=[vmem] * len(moving),
            scratch_shapes=[
                pltpu.SMEM((count,), jnp.int32),
                pltpu.SemaphoreType.DMA((2 * (width // LANES),)),
            ],
            input_output_aliases={lead + at: at for at in range(len(state))},
            compiler_params=pltpu.CompilerParams(
                vmem_limit_bytes=VMEM_LIMIT
            ),
            cost_estimate=pl.CostEstimate(
                flops=8 * count * length**3,
                bytes_accessed=8 * tile_px * tile_px,
                transcendentals=0,
            ),
            name=f"patches_{phase}",
        )(corners, *more, *held, *state)
    return state[0], state[2], held


def fit_scalars(materials_ref, energies, kinds):
    spectra = [
        [materials_ref[part, energy, kind] for kind in range(kinds)]
        for part in range(2)
        for energy in range(energies)
    ]
    gram = [[None] * kinds for _ in range(kinds)]
    for one in range(kinds):
        for other in range(one, kinds):
            total = spectra[0][one] * spectra[0][other]
            for row in spectra[1:]:
                total = total + row[one] * row[other]
            gram[one][other] = total
            gram[other][one] = total
    trace = gram[0][0]
    for one in range(1, kinds):
        trace = trace + gram[one][one]
    return gram, trace


def fit_columns(materials_ref, step_ref, data, spectra, energies, kinds, rate, begin, wide):
    rows = data.shape[2]
    tall = 16 if rows % 16 == 0 else 8
    pairs = [(part, energy) for part in range(2) for energy in range(energies)]

    def chunk(number, carry):
        row = pl.multiple_of(number * tall, tall)
        place = (pl.ds(row, tall), pl.ds(begin, wide))
        target = [None] * kinds
        for part, energy in pairs:
            plane = data[(part, energy) + place]
            for kind in range(kinds):
                term = materials_ref[part, energy, kind] * plane
                target[kind] = term if target[kind] is None else target[kind] + term
        target = [rate * value for value in target]
        current = [jnp.maximum(value, 0.0) for value in target]

        def descend(turn, current):
            following = []
            for one in range(kinds):
                total = target[one]
                for other in range(kinds):
                    total = total + step_ref[one * kinds + other] * current[other]
                following.append(jnp.maximum(total, 0.0))
            return following

        current = lax.fori_loop(1, FIT_STEPS, descend, current)
        for part, energy in pairs:
            total = None
            for kind in range(kinds):
                term = materials_ref[part, energy, kind] * current[kind]
                total = term if total is None else total + term
            spectra[(part, energy) + place] = total
        return carry

    lax.fori_loop(0, rows // tall, chunk, 0)


def exchange_kernel(
    groups,
    tiles,
    fold,
    materials_ref,
    corners_ref,
    gradient,
    field,
    held,
    left_table,
    right_table,
    probe,
    split,
    out_ref,
    step_ref,
    order,
    wave,
    change,
    terms,
    padded,
    added,
    main,
    side,
    margin,
    data,
    spectra,
    margin_sems,
    send_sems,
    recv_sems,
    own_sems,
):
    mesh_ids = pl.DeviceIdType.MESH
    me = lax.axis_index("energy")
    tile = lax.axis_index("tile")
    after = lax.rem(tile + 1, tiles)
    before = lax.rem(tile + tiles - 1, tiles)
    tile_px = out_ref.shape[-1]
    length = probe.shape[2]
    blocks = tile_px // LANES
    rows = tile_px // groups
    kinds = materials_ref.shape[2]
    offsets = sorted(range(1, groups), key=lambda offset: abs(offset - groups // 2))
    peers = {offset: lax.rem(me + offset, groups) for offset in offsets}

    barrier = pltpu.get_barrier_semaphore()
    pl.semaphore_signal(barrier, inc=1, device_id=(me, before), device_id_type=mesh_ids)
    for offset in offsets:
        pl.semaphore_signal(
            barrier, inc=1, device_id=(peers[offset], tile), device_id_type=mesh_ids
        )

    peak = jnp.max(probe[0] * probe[0] + probe[1] * probe[1])
    tall = 64
    inverse = 1.0 / jnp.full((tall, LANES), peak, jnp.float32)

    width = field.shape[1]
    pieces = width - blocks
    count = held.shape[0]
    slots = late_count(count, fold)
    early = [block for block in range(blocks) if block * LANES >= length]
    late = [block for block in range(blocks) if block * LANES < length]
    touched = list(range(blocks - 1, width)) if slots else list(range(blocks, width))
    firsts = [block for block in early if block not in touched]

    def finish_rows(which, wrapped, number, carry):
        place = (pl.ds(pl.multiple_of(number * tall, tall), tall), slice(None))
        beyond = pl.ds(pl.multiple_of(tile_px + number * tall, tall), tall)
        for part in range(2):
            for block in which:
                value = gradient[(part, block) + place]
                if wrapped:
                    value = value + gradient[part, block, beyond, :]
                if slots and block in touched:
                    value = value + added[(part, block - blocks + 1) + place]
                share = value * inverse
                if block < blocks:
                    main[(part, block) + place] = field[(part, block) + place] + share
                else:
                    side[(part, block - blocks) + place] = share
        return carry

    def finish(which):
        lax.fori_loop(0, length // tall, functools.partial(finish_rows, which, fold), 0)
        lax.fori_loop(
            length // tall, tile_px // tall, functools.partial(finish_rows, which, False), 0
        )

    def late_patches():
        phases = 1 + pieces
        spots, ends = patch_order(corners_ref, count, phases, tile_px - length, fold)
        for slot in range(slots):
            order[slot] = sum(
                jnp.where(spot == count - 1 - slot, number, 0) for number, spot in enumerate(spots)
            )
        corner, gather, outward, keep, homeward = patch_stages(
            corners_ref, order, field, held, left_table, right_table, probe, split, wave, change
        )
        padded[...] = jnp.zeros_like(padded)
        added[...] = jnp.zeros_like(added)
        terms[...] = jnp.zeros_like(terms)
        lane = lax.broadcasted_iota(jnp.int32, (length, LANES), 1)

        def place(turn):
            _, row, _, shift = corner(turn)
            at_most = lane >= shift
            for part in range(2):
                tiles = [
                    pltpu.roll(terms[part, :, at : at + LANES], shift, 1)
                    for at in range(0, length, LANES)
                ]
                zero = jnp.zeros_like(tiles[0])
                for at, (one, other) in enumerate(zip(tiles + [zero], [zero] + tiles)):
                    value = jnp.where(at_most, one, other)
                    padded[part, at, :length] = value
                    padded[part, at, tile_px : tile_px + length] = value
                    moved = padded[part, at, pl.ds(tile_px - row, tile_px), :]
                    added[part, at] = added[part, at] + moved

        def leave(turn, back):
            valid = count - 1 - turn >= ends[phases - 2]
            terms[0] = jnp.where(valid, back[0], 0.0)
            terms[1] = jnp.where(valid, back[1], 0.0)

        def step(turn, carry):
            place(jnp.maximum(turn - 1, 0))
            parts = outward(turn + 1)
            back = homeward()
            keep(parts)
            gather(jnp.minimum(turn + 2, slots - 1))
            leave(turn, back)
            return carry

        gather(0)
        keep(outward(0))
        gather(min(1, slots - 1))
        lax.fori_loop(0, slots - 1, step, 0)
        place(max(slots - 2, 0))
        leave(slots - 1, homeward())
        place(slots - 1)

    finish(firsts)

    pl.semaphore_wait(barrier, groups)

    margin_copy = pltpu.make_async_remote_copy(
        src_ref=side,
        dst_ref=margin,
        send_sem=margin_sems.at[0],
        recv_sem=margin_sems.at[1],
        device_id=(me, after),
        device_id_type=mesh_ids,
    )
    def rows_of(group):
        return pl.ds(pl.multiple_of(group * rows, rows), rows)

    def outward(block):
        columns = pl.ds(block * LANES, LANES)
        copies = [
            pltpu.make_async_remote_copy(
                src_ref=main.at[:, block, rows_of(peers[offset]), :],
                dst_ref=data.at[:, me, :, columns],
                send_sem=send_sems.at[0, block, offset],
                recv_sem=recv_sems.at[0, block, offset],
                device_id=(peers[offset], tile),
                device_id_type=mesh_ids,
            )
            for offset in offsets
        ]
        own = pltpu.make_async_copy(
            main.at[:, block, rows_of(me), :], data.at[:, me, :, columns], own_sems.at[0, block]
        )
        return copies, own

    def homeward(block):
        columns = pl.ds(block * LANES, LANES)
        copies = [
            pltpu.make_async_remote_copy(
                src_ref=spectra.at[:, peers[offset], :, columns],
                dst_ref=out_ref.at[:, rows_of(me), columns],
                send_sem=send_sems.at[1, block, offset],
                recv_sem=recv_sems.at[1, block, offset],
                device_id=(peers[offset], tile),
                device_id_type=mesh_ids,
            )
            for offset in offsets
        ]
        own = pltpu.make_async_copy(
            spectra.at[:, me, :, columns], out_ref.at[:, rows_of(me), columns], own_sems.at[1, block]
        )
        return copies, own

    def start(moves):
        for copy in moves[0]:
            copy.start()
        moves[1].start()

    going = {}
    coming = {}

    def send(which):
        for block in which:
            going[block] = outward(block)
            start(going[block])

    def settle(which):
        for block in which:
            copies, own = going[block]
            for copy in copies:
                copy.wait_recv()
            own.wait()
            fit_columns(
                materials_ref, step_ref, data, spectra, groups, kinds, rate, block * LANES, LANES
            )
            coming[block] = homeward(block)
            start(coming[block])

    send(firsts)
    if slots:
        late_patches()
    edges = [block for block in touched if block < blocks]
    finish(touched)
    margin_copy.start()
    send(edges)
    finish(late)
    gram, trace = fit_scalars(materials_ref, groups, kinds)
    rate = 1.0 / trace
    for one in range(kinds):
        for other in range(kinds):
            unit = 1.0 if one == other else 0.0
            step_ref[one * kinds + other] = unit - rate * gram[one][other]
    settle(firsts)
    margin_copy.wait()
    for block in late:
        main[:, block] = main[:, block] + margin[:, block]
    send(late)
    settle(edges + late)
    for block in firsts + edges + late:
        for copy in going[block][0]:
            copy.wait_send()
        copies, own = coming[block]
        own.wait()
        for copy in copies:
            copy.wait()


def exchange_fit(gradient, field, held, corners, materials, fold):
    groups = lax.axis_size("energy")
    tiles = lax.axis_size("tile")
    pieces = held[3].shape[1]
    length = held[3].shape[2]
    blocks = field.shape[1] - pieces
    tile_px = blocks * LANES
    kinds = materials.shape[-1]
    rows = tile_px // groups
    vmem = pl.BlockSpec(memory_space=pltpu.VMEM)
    return pl.pallas_call(
        functools.partial(exchange_kernel, groups, tiles, fold),
        out_shape=jax.ShapeDtypeStruct((2, tile_px, tile_px), jnp.float32),
        in_specs=[pl.BlockSpec(memory_space=pltpu.SMEM)] * 2 + [vmem] * (2 + len(held)),
        out_specs=vmem,
        scratch_shapes=[
            pltpu.SMEM((kinds * kinds,), jnp.float32),
            pltpu.SMEM((max(LATE, 1),), jnp.int32),
            pltpu.VMEM((2, length, length), jnp.bfloat16),
            pltpu.VMEM((2, pieces, length, LANES), jnp.float32),
            pltpu.VMEM((2, length, length), jnp.float32),
            pltpu.VMEM((2, pieces + 1, 2 * tile_px, LANES), jnp.float32),
            pltpu.VMEM((2, pieces + 1, tile_px, LANES), jnp.float32),
            pltpu.VMEM((2, blocks, tile_px, LANES), jnp.float32),
            pltpu.VMEM((2, pieces, tile_px, LANES), jnp.float32),
            pltpu.VMEM((2, pieces, tile_px, LANES), jnp.float32),
            pltpu.VMEM((2, groups, rows, tile_px), jnp.float32),
            pltpu.VMEM((2, groups, rows, tile_px), jnp.float32),
            pltpu.SemaphoreType.DMA((2,)),
            pltpu.SemaphoreType.DMA((2, blocks, groups)),
            pltpu.SemaphoreType.DMA((2, blocks, groups)),
            pltpu.SemaphoreType.DMA((2, blocks)),
        ],
        compiler_params=pltpu.CompilerParams(
            collective_id=0,
            has_side_effects=True,
            vmem_limit_bytes=24 * 1024 * 1024,
        ),
        name="exchange",
    )(materials, corners, gradient, field, *held)


def body(object_tiles, probe_wave, measured, positions, materials):
    own_object = object_tiles[0, :, 0]
    tile_px = own_object.shape[-1]
    length = probe_wave.shape[-1]
    row_step = TILE_COLS % lax.axis_size("tile")
    fold = row_step == 0
    gradient, field, held = patch_calls(
        own_object,
        probe_wave[0],
        measured[0, 0],
        positions[0].T,
        fold,
        functools.partial(shifted, axis="tile", steps=-1),
    )
    if not fold:
        from_above = shifted(gradient[:, :, tile_px:], "tile", row_step)
        gradient = gradient.at[:, :, :length].add(from_above)
    fitted = exchange_fit(gradient, field, held, positions[0].T, materials, fold)
    return fitted.reshape(1, 2, 1, tile_px, tile_px)


def solution(mesh):
    in_specs = (
        P("energy", None, "tile", None, None),
        P("energy", None, None, None),
        P("energy", "tile", None, None, None),
        P("tile", None, None),
        P(),
    )
    out_specs = P("energy", None, "tile", None, None)
    return jax.shard_map(body, mesh=mesh, in_specs=in_specs, out_specs=out_specs, check_vma=False)
```

```python
import functools
import math

import jax
import jax.numpy as jnp
import numpy as np
from jax import lax
from jax.experimental import pallas as pl
from jax.experimental.pallas import tpu as pltpu
from jax.sharding import PartitionSpec as P

TILE_COLS = 4
FIT_STEPS = 10
LANES = 128
LATE = 8
VMEM_LIMIT = 12 * 1024 * 1024
LOAD_LIMIT = 8 * 1024 * 1024


amplitude_floor = 0.5


def shifted(value, axis, steps):
    count = lax.axis_size(axis)
    pairs = [(source, (source + steps) % count) for source in range(count)]
    return lax.ppermute(value, axis, pairs)


def trig_parts(rows, columns, length):
    angles = 2.0 * math.pi / length * (rows[:, None] * columns[None, :] % length)
    return np.stack([np.cos(angles), np.sin(angles)]).astype(np.float32).astype(jnp.bfloat16)


def fourier_parts(length):
    counter = np.arange(length, dtype=np.int64)
    half = counter[: length // 2]
    left = np.stack([trig_parts(half, counter[parity::2], length) for parity in range(2)])
    return jnp.asarray(left), jnp.asarray(trig_parts(counter, counter, length))


def joined(top_left, top_right, bottom_left, bottom_right):
    return jnp.concatenate(
        [
            jnp.concatenate([top_left, top_right], 1),
            jnp.concatenate([bottom_left, bottom_right], 1),
        ],
        0,
    )


def transform(even, odd, left_ref, right_ref):
    length = even.shape[0]
    half = length // 2
    one = jnp.dot(left_ref[0], even, preferred_element_type=jnp.float32)
    two = jnp.dot(left_ref[1], odd, preferred_element_type=jnp.float32)
    upper = (one + two).astype(jnp.bfloat16)
    lower = (one - two).astype(jnp.bfloat16)
    beside = joined(upper[:half], upper[half:], lower[:half], lower[half:])
    outer = jnp.dot(beside, right_ref[...], preferred_element_type=jnp.float32)
    return outer[:, :length], outer[:, length:]


def window(ref, part, rows, block, shift, length):
    lane = lax.broadcasted_iota(jnp.int32, (rows.size, LANES), 1)
    back = lax.rem(LANES - shift, LANES)
    tiles = [
        pltpu.roll(ref[part, block + at, rows, :], back, 1) for at in range(length // LANES + 1)
    ]
    keep = lane < LANES - shift
    return jnp.concatenate(
        [jnp.where(keep, one, other) for one, other in zip(tiles[:-1], tiles[1:])], 1
    )


def add_window(ref, part, row, block, shift, term):
    length = term.shape[0]
    lane = lax.broadcasted_iota(jnp.int32, (length, LANES), 1)
    tiles = [pltpu.roll(term[:, at : at + LANES], shift, 1) for at in range(0, length, LANES)]
    keep = lane >= shift
    zero = jnp.zeros_like(tiles[0])
    for at, (one, other) in enumerate(zip(tiles + [zero], [zero] + tiles)):
        place = (part, block + at, pl.ds(row, length), slice(None))
        ref[place] = ref[place] + jnp.where(keep, one, other)


def load_kernel(object_ref, probe_ref, left_ref, right_ref, *refs):
    *strips, gradient, terms, left, right, probe, split = refs[:-3]
    parts_left, parts_right, sems = refs[-3:]
    length = probe_ref.shape[-1]
    half = length // 2
    pieces = length // LANES
    moves = [(left_ref, parts_left), (right_ref, parts_right)]
    for piece, strip in enumerate(strips):
        moves.append((object_ref.at[:, :, pl.ds(piece * LANES, LANES)], strip))
    for piece in range(pieces):
        columns = pl.ds(piece * LANES, LANES)
        moves.append((probe_ref.at[:, :, columns], probe.at[:, piece]))
    copies = [
        pltpu.make_async_copy(source, target, sems.at[number])
        for number, (source, target) in enumerate(moves)
    ]
    for copy in copies:
        copy.start()
    gradient[...] = jnp.zeros_like(gradient)
    terms[...] = jnp.zeros_like(terms)
    for copy in copies[:2]:
        copy.wait()
    for parity in range(2):
        cosine = parts_left[parity, 0]
        sine = parts_left[parity, 1]
        left[0, parity] = joined(cosine, sine, -sine, cosine)
        left[1, parity] = joined(cosine, -sine, sine, cosine)
    scale = jnp.asarray(1.0 / length, jnp.bfloat16)
    cosine = parts_right[0] * scale
    sine = parts_right[1] * scale
    right[0] = joined(cosine, -sine, sine, cosine)
    right[1] = joined(cosine, sine, -sine, cosine)
    for copy in copies[2:]:
        copy.wait()
    for parity in range(2):
        for part in range(2):
            for piece in range(pieces):
                columns = slice(piece * LANES, (piece + 1) * LANES)
                rows = pl.ds(parity, half, stride=2)
                split[parity, part, :, columns] = probe[part, piece, rows, :]


def patch_stages(corners_ref, order, field, held, left, right, probe, split, wave, change):
    length = wave.shape[-1]
    half = length // 2
    pieces = length // LANES

    def corner(turn):
        number = order[turn]
        row = corners_ref[0, number]
        col = corners_ref[1, number]
        block = col // LANES
        return number, row, block, col - block * LANES

    def gather(turn):
        _, row, block, shift = corner(turn)
        for parity in range(2):
            rows = pl.ds(row + parity, half, stride=2)
            piece_real = window(field, 0, rows, block, shift, length)
            piece_imag = window(field, 1, rows, block, shift, length)
            probe_real = split[parity, 0]
            probe_imag = split[parity, 1]
            exit_real = probe_real * piece_real - probe_imag * piece_imag
            exit_imag = probe_real * piece_imag + probe_imag * piece_real
            wave[parity, :half, :] = exit_real.astype(jnp.bfloat16)
            wave[parity, half:, :] = exit_imag.astype(jnp.bfloat16)

    def outward(turn):
        far_real, far_imag = transform(wave[0], wave[1], left.at[0], right.at[0])
        square = far_real * far_real + far_imag * far_imag
        scale = lax.rsqrt(jnp.maximum(square, amplitude_floor * amplitude_floor))
        factor = held[order[turn]].astype(jnp.float32) * scale - 1.0
        return factor * far_real, factor * far_imag

    def keep(parts):
        for part in range(2):
            for piece in range(pieces):
                change[part, piece] = parts[part][:, piece * LANES : (piece + 1) * LANES]

    def changed(parity):
        rows = pl.ds(parity, half, stride=2)
        return jnp.concatenate(
            [
                jnp.concatenate([change[part, piece, rows, :] for piece in range(pieces)], 1)
                for part in range(2)
            ],
            0,
        ).astype(jnp.bfloat16)

    def homeward():
        back_real, back_imag = transform(changed(0), changed(1), left.at[1], right.at[1])
        probe_real = jnp.concatenate([probe[0, piece] for piece in range(pieces)], 1)
        probe_imag = jnp.concatenate([probe[1, piece] for piece in range(pieces)], 1)
        return (
            probe_real * back_real + probe_imag * back_imag,
            probe_real * back_imag - probe_imag * back_real,
        )

    return corner, gather, outward, keep, homeward


def patch_order(corners_ref, count, phases, limit, fold):
    def rank(number):
        beyond = corners_ref[1, number] - limit
        kind = sum(jnp.where(beyond > step * LANES, 8, 0) for step in range(phases - 1))
        if not fold:
            kind = jnp.where(corners_ref[0, number] > limit, 8 * (phases - 1), kind)
        return kind

    kinds = [rank(number) for number in range(count)]
    total = sum(jnp.left_shift(1, kind) for kind in kinds)
    place = sum(jnp.left_shift(total, 8 * step) for step in range(1, phases))
    ends = [
        lax.bitwise_and(jnp.right_shift(total + place, 8 * step), 255) for step in range(phases)
    ]
    spots = []
    for kind in kinds:
        spots.append(lax.bitwise_and(jnp.right_shift(place, kind), 255))
        place = place + jnp.left_shift(1, kind)
    return spots, ends


def late_count(count, fold):
    return min(LATE, count) if fold else 0


def patch_kernel(fold, phase, phases, *refs):
    first = phase == 0
    last = phase == phases - 1
    lower_count = 1 if last and not fold else 0
    lead = 2 + lower_count
    corners_ref = refs[0]
    source_ref = refs[1]
    lower_ref = refs[2] if lower_count else None
    held, left, right, probe, split = refs[lead : lead + 5]
    refs = refs[lead + 5 + (2 if first else 5) :]
    gradient, terms, field, wave, change = refs[:5]
    order, sems = refs[-2:]
    length = wave.shape[-1]
    half = length // 2
    pieces = length // LANES
    width = field.shape[1]
    blocks = width - pieces
    tile_px = blocks * LANES
    count = held.shape[0]
    limit = tile_px - length
    top = pl.ds(0, tile_px)
    bottom = pl.ds(tile_px, length)
    moves = []
    if first:
        for block in range(blocks):
            columns = pl.ds(block * LANES, LANES)
            moves.append((source_ref.at[:, :, columns], field.at[:, block, top, :]))
            if fold:
                source = source_ref.at[:, pl.ds(0, length), columns]
                moves.append((source, field.at[:, block, bottom, :]))
    elif last and not fold:
        for block in range(width):
            columns = pl.ds(block * LANES, LANES)
            moves.append((lower_ref.at[:, :, columns], field.at[:, block, bottom, :]))
    copies = [
        pltpu.make_async_copy(source, target, sems.at[number])
        for number, (source, target) in enumerate(moves)
    ]
    for copy in copies:
        copy.start()

    if not first:
        for part in range(2):
            strip = source_ref[part]
            field[part, blocks + phase - 1, :tile_px] = strip
            if fold:
                field[part, blocks + phase - 1, tile_px:] = strip[:length]
    spots, ends = patch_order(corners_ref, count, phases, limit, fold)

    def fill_order():
        for number, spot in enumerate(spots):
            order[spot] = number

    if not last:
        fill_order()
    for copy in copies:
        copy.wait()
    corner, gather, outward, keep, homeward = patch_stages(
        corners_ref, order, field, held, left, right, probe, split, wave, change
    )

    def scatter(turn):
        _, row, block, shift = corner(turn)
        add_window(gradient, 0, row, block, shift, terms[0])
        add_window(gradient, 1, row, block, shift, terms[1])

    def leave(turn):
        back = homeward()
        terms[0] = back[0]
        terms[1] = back[1]

    def step(low, high, turn, carry):
        scatter(jnp.maximum(turn - 1, low))
        parts = outward(turn + 1)
        back = homeward()
        keep(parts)
        gather(jnp.minimum(turn + 2, high - 1))
        terms[0] = back[0]
        terms[1] = back[1]
        return carry

    def enter(low, high):
        gather(low)
        keep(outward(low))
        gather(jnp.minimum(low + 1, high - 1))

    def drain(low, high):
        scatter(jnp.maximum(high - 2, low))
        leave(high - 1)
        scatter(high - 1)

    if last:
        low = ends[phases - 2]
        high = jnp.maximum(low, count - late_count(count, fold))

        @pl.when(high > low)
        def _():
            fill_order()
            terms[...] = jnp.zeros_like(terms)
            enter(low, high)
            lax.fori_loop(low, high - 1, functools.partial(step, low, high), 0)
            drain(low, high)

        return
    draining = phase == phases - 2
    high = ends[phase]
    before = ends[phase - 1] if phase else 0
    enough = 1 if draining else 2

    @pl.when(jnp.logical_and(high >= enough, before < 2))
    def _():
        enter(0, high)

    begin = jnp.maximum(before - 2, 0)
    end = high - 1 if draining else jnp.maximum(high - 2, 0)
    lax.fori_loop(begin, end, functools.partial(step, 0, high), 0)
    if draining:

        @pl.when(high > 0)
        def _():
            drain(0, high)


def patch_calls(own_object, probe, measured, corners, fold, shift):
    tile_px = own_object.shape[-1]
    length = probe.shape[-1]
    count = measured.shape[0]
    width = tile_px + length
    pieces = length // LANES
    phases = 1 + pieces
    vmem = pl.BlockSpec(memory_space=pltpu.VMEM)
    anywhere = pl.BlockSpec(memory_space=pl.ANY)
    smem = pl.BlockSpec(memory_space=pltpu.SMEM)

    def single(*shape):
        return jax.ShapeDtypeStruct(shape, jnp.float32)

    def brief(*shape):
        return jax.ShapeDtypeStruct(shape, jnp.bfloat16)

    sums = (2, width // LANES, width, LANES)
    moving = [
        single(*sums),
        single(2, length, length),
        single(*sums),
        brief(2, length, length),
        single(2, pieces, length, LANES),
    ]
    fixed = [
        brief(2, 2, length, length),
        brief(2, 2 * length, 2 * length),
        single(2, pieces, length, LANES),
        single(2, 2, length // 2, length),
    ]
    loaded = [single(2, tile_px, LANES)] * pieces + moving[:2] + fixed
    parts_left, parts_right = fourier_parts(length)
    sources = (own_object, probe, parts_left, parts_right)
    out = pl.pallas_call(
        load_kernel,
        out_shape=loaded,
        in_specs=[anywhere] * 4,
        out_specs=[vmem] * len(loaded),
        scratch_shapes=[
            pltpu.VMEM(parts_left.shape, jnp.bfloat16),
            pltpu.VMEM(parts_right.shape, jnp.bfloat16),
            pltpu.SemaphoreType.DMA((2 + 2 * pieces,)),
        ],
        compiler_params=pltpu.CompilerParams(vmem_limit_bytes=LOAD_LIMIT),
        cost_estimate=pl.CostEstimate(flops=10**10, bytes_accessed=2**24, transcendentals=0),
        name="load",
    )(*(pltpu.with_memory_space_constraint(value, pltpu.HBM) for value in sources))
    strips = [shift(strip) for strip in out[:pieces]]
    state = list(out[pieces : pieces + 2])
    held = [measured, *out[pieces + 2 :]]
    for phase in range(phases):
        last = phase == phases - 1
        more = [strips[phase - 1] if phase else own_object]
        if last and not fold:
            widened = jnp.concatenate(
                [own_object[:, :length]] + [strip[:, :length] for strip in strips], 2
            )
            more.append(shifted(widened, "tile", -(TILE_COLS % lax.axis_size("tile"))))
        lead = 1 + len(more) + len(held)
        state = pl.pallas_call(
            functools.partial(patch_kernel, fold, phase, phases),
            out_shape=moving,
            in_specs=[smem]
            + [vmem if phase else anywhere]
            + [anywhere] * (len(more) - 1)
            + [vmem] * (len(held) + len(state)),
            out_specs=[vmem] * len(moving),
            scratch_shapes=[
                pltpu.SMEM((count,), jnp.int32),
                pltpu.SemaphoreType.DMA((2 * (width // LANES),)),
            ],
            input_output_aliases={lead + at: at for at in range(len(state))},
            compiler_params=pltpu.CompilerParams(
                vmem_limit_bytes=VMEM_LIMIT
            ),
            cost_estimate=pl.CostEstimate(
                flops=8 * count * length**3,
                bytes_accessed=8 * tile_px * tile_px,
                transcendentals=0,
            ),
            name=f"patches_{phase}",
        )(corners, *more, *held, *state)
    return state[0], state[2], held


def fit_scalars(materials_ref, energies, kinds):
    spectra = [
        [materials_ref[part, energy, kind] for kind in range(kinds)]
        for part in range(2)
        for energy in range(energies)
    ]
    gram = [[None] * kinds for _ in range(kinds)]
    for one in range(kinds):
        for other in range(one, kinds):
            total = spectra[0][one] * spectra[0][other]
            for row in spectra[1:]:
                total = total + row[one] * row[other]
            gram[one][other] = total
            gram[other][one] = total
    trace = gram[0][0]
    for one in range(1, kinds):
        trace = trace + gram[one][one]
    return gram, trace


def fit_columns(materials_ref, step_ref, data, spectra, energies, kinds, rate, begin, wide):
    rows = data.shape[2]
    tall = 16 if rows % 16 == 0 else 8
    pairs = [(part, energy) for part in range(2) for energy in range(energies)]

    def chunk(number, carry):
        row = pl.multiple_of(number * tall, tall)
        place = (pl.ds(row, tall), pl.ds(begin, wide))
        target = [None] * kinds
        for part, energy in pairs:
            plane = data[(part, energy) + place]
            for kind in range(kinds):
                term = materials_ref[part, energy, kind] * plane
                target[kind] = term if target[kind] is None else target[kind] + term
        target = [rate * value for value in target]
        current = [jnp.maximum(value, 0.0) for value in target]

        def descend(turn, current):
            following = []
            for one in range(kinds):
                total = target[one]
                for other in range(kinds):
                    total = total + step_ref[one * kinds + other] * current[other]
                following.append(jnp.maximum(total, 0.0))
            return following

        current = lax.fori_loop(1, FIT_STEPS, descend, current)
        for part, energy in pairs:
            total = None
            for kind in range(kinds):
                term = materials_ref[part, energy, kind] * current[kind]
                total = term if total is None else total + term
            spectra[(part, energy) + place] = total
        return carry

    lax.fori_loop(0, rows // tall, chunk, 0)


def exchange_kernel(
    groups,
    tiles,
    fold,
    materials_ref,
    corners_ref,
    gradient,
    field,
    held,
    left_table,
    right_table,
    probe,
    split,
    out_ref,
    step_ref,
    order,
    wave,
    change,
    terms,
    padded,
    added,
    main,
    side,
    margin,
    data,
    spectra,
    margin_sems,
    send_sems,
    recv_sems,
    own_sems,
):
    mesh_ids = pl.DeviceIdType.MESH
    me = lax.axis_index("energy")
    tile = lax.axis_index("tile")
    after = lax.rem(tile + 1, tiles)
    before = lax.rem(tile + tiles - 1, tiles)
    tile_px = out_ref.shape[-1]
    length = probe.shape[2]
    blocks = tile_px // LANES
    rows = tile_px // groups
    kinds = materials_ref.shape[2]
    offsets = sorted(range(1, groups), key=lambda offset: abs(offset - groups // 2))
    peers = {offset: lax.rem(me + offset, groups) for offset in offsets}

    barrier = pltpu.get_barrier_semaphore()
    pl.semaphore_signal(barrier, inc=1, device_id=(me, before), device_id_type=mesh_ids)
    for offset in offsets:
        pl.semaphore_signal(
            barrier, inc=1, device_id=(peers[offset], tile), device_id_type=mesh_ids
        )

    peak = jnp.max(probe[0] * probe[0] + probe[1] * probe[1])
    tall = 64
    inverse = 1.0 / jnp.full((tall, LANES), peak, jnp.float32)

    width = field.shape[1]
    pieces = width - blocks
    count = held.shape[0]
    slots = late_count(count, fold)
    early = [block for block in range(blocks) if block * LANES >= length]
    late = [block for block in range(blocks) if block * LANES < length]
    touched = list(range(blocks - 1, width)) if slots else list(range(blocks, width))
    firsts = [block for block in early if block not in touched]

    def finish_rows(which, wrapped, number, carry):
        place = (pl.ds(pl.multiple_of(number * tall, tall), tall), slice(None))
        beyond = pl.ds(pl.multiple_of(tile_px + number * tall, tall), tall)
        for part in range(2):
            for block in which:
                value = gradient[(part, block) + place]
                if wrapped:
                    value = value + gradient[part, block, beyond, :]
                if slots and block in touched:
                    value = value + added[(part, block - blocks + 1) + place]
                share = value * inverse
                if block < blocks:
                    main[(part, block) + place] = field[(part, block) + place] + share
                else:
                    side[(part, block - blocks) + place] = share
        return carry

    def finish(which):
        lax.fori_loop(0, length // tall, functools.partial(finish_rows, which, fold), 0)
        lax.fori_loop(
            length // tall, tile_px // tall, functools.partial(finish_rows, which, False), 0
        )

    def late_patches():
        phases = 1 + pieces
        spots, ends = patch_order(corners_ref, count, phases, tile_px - length, fold)
        for slot in range(slots):
            order[slot] = sum(
                jnp.where(spot == count - 1 - slot, number, 0) for number, spot in enumerate(spots)
            )
        corner, gather, outward, keep, homeward = patch_stages(
            corners_ref, order, field, held, left_table, right_table, probe, split, wave, change
        )
        padded[...] = jnp.zeros_like(padded)
        added[...] = jnp.zeros_like(added)
        terms[...] = jnp.zeros_like(terms)
        lane = lax.broadcasted_iota(jnp.int32, (length, LANES), 1)

        def place(turn):
            _, row, _, shift = corner(turn)
            at_most = lane >= shift
            for part in range(2):
                tiles = [
                    pltpu.roll(terms[part, :, at : at + LANES], shift, 1)
                    for at in range(0, length, LANES)
                ]
                zero = jnp.zeros_like(tiles[0])
                for at, (one, other) in enumerate(zip(tiles + [zero], [zero] + tiles)):
                    value = jnp.where(at_most, one, other)
                    padded[part, at, :length] = value
                    padded[part, at, tile_px : tile_px + length] = value
                    moved = padded[part, at, pl.ds(tile_px - row, tile_px), :]
                    added[part, at] = added[part, at] + moved

        def leave(turn, back):
            valid = count - 1 - turn >= ends[phases - 2]
            terms[0] = jnp.where(valid, back[0], 0.0)
            terms[1] = jnp.where(valid, back[1], 0.0)

        def step(turn, carry):
            place(jnp.maximum(turn - 1, 0))
            parts = outward(turn + 1)
            back = homeward()
            keep(parts)
            gather(jnp.minimum(turn + 2, slots - 1))
            leave(turn, back)
            return carry

        gather(0)
        keep(outward(0))
        gather(min(1, slots - 1))
        lax.fori_loop(0, slots - 1, step, 0)
        place(max(slots - 2, 0))
        leave(slots - 1, homeward())
        place(slots - 1)

    finish(firsts)

    pl.semaphore_wait(barrier, groups)

    margin_copy = pltpu.make_async_remote_copy(
        src_ref=side,
        dst_ref=margin,
        send_sem=margin_sems.at[0],
        recv_sem=margin_sems.at[1],
        device_id=(me, after),
        device_id_type=mesh_ids,
    )
    def rows_of(group):
        return pl.ds(pl.multiple_of(group * rows, rows), rows)

    def outward(block):
        columns = pl.ds(block * LANES, LANES)
        copies = [
            pltpu.make_async_remote_copy(
                src_ref=main.at[:, block, rows_of(peers[offset]), :],
                dst_ref=data.at[:, me, :, columns],
                send_sem=send_sems.at[0, block, offset],
                recv_sem=recv_sems.at[0, block, offset],
                device_id=(peers[offset], tile),
                device_id_type=mesh_ids,
            )
            for offset in offsets
        ]
        own = pltpu.make_async_copy(
            main.at[:, block, rows_of(me), :], data.at[:, me, :, columns], own_sems.at[0, block]
        )
        return copies, own

    def homeward(block):
        columns = pl.ds(block * LANES, LANES)
        copies = [
            pltpu.make_async_remote_copy(
                src_ref=spectra.at[:, peers[offset], :, columns],
                dst_ref=out_ref.at[:, rows_of(me), columns],
                send_sem=send_sems.at[1, block, offset],
                recv_sem=recv_sems.at[1, block, offset],
                device_id=(peers[offset], tile),
                device_id_type=mesh_ids,
            )
            for offset in offsets
        ]
        own = pltpu.make_async_copy(
            spectra.at[:, me, :, columns], out_ref.at[:, rows_of(me), columns], own_sems.at[1, block]
        )
        return copies, own

    def start(moves):
        for copy in moves[0]:
            copy.start()
        moves[1].start()

    going = {}
    coming = {}

    def send(which):
        for block in which:
            going[block] = outward(block)
            start(going[block])

    def settle(which):
        for block in which:
            copies, own = going[block]
            for copy in copies:
                copy.wait_recv()
            own.wait()
            fit_columns(
                materials_ref, step_ref, data, spectra, groups, kinds, rate, block * LANES, LANES
            )
            coming[block] = homeward(block)
            start(coming[block])

    send(firsts)
    if slots:
        late_patches()
    edges = [block for block in touched if block < blocks]
    finish(touched)
    margin_copy.start()
    send(edges)
    finish(late)
    gram, trace = fit_scalars(materials_ref, groups, kinds)
    rate = 1.0 / trace
    for one in range(kinds):
        for other in range(kinds):
            unit = 1.0 if one == other else 0.0
            step_ref[one * kinds + other] = unit - rate * gram[one][other]
    settle(firsts)
    margin_copy.wait()
    for block in late:
        main[:, block] = main[:, block] + margin[:, block]
    send(late)
    settle(edges + late)
    for block in firsts + edges + late:
        for copy in going[block][0]:
            copy.wait_send()
        copies, own = coming[block]
        own.wait()
        for copy in copies:
            copy.wait()


def exchange_fit(gradient, field, held, corners, materials, fold):
    groups = lax.axis_size("energy")
    tiles = lax.axis_size("tile")
    pieces = held[3].shape[1]
    length = held[3].shape[2]
    blocks = field.shape[1] - pieces
    tile_px = blocks * LANES
    kinds = materials.shape[-1]
    rows = tile_px // groups
    vmem = pl.BlockSpec(memory_space=pltpu.VMEM)
    return pl.pallas_call(
        functools.partial(exchange_kernel, groups, tiles, fold),
        out_shape=jax.ShapeDtypeStruct((2, tile_px, tile_px), jnp.float32),
        in_specs=[pl.BlockSpec(memory_space=pltpu.SMEM)] * 2 + [vmem] * (2 + len(held)),
        out_specs=vmem,
        scratch_shapes=[
            pltpu.SMEM((kinds * kinds,), jnp.float32),
            pltpu.SMEM((max(LATE, 1),), jnp.int32),
            pltpu.VMEM((2, length, length), jnp.bfloat16),
            pltpu.VMEM((2, pieces, length, LANES), jnp.float32),
            pltpu.VMEM((2, length, length), jnp.float32),
            pltpu.VMEM((2, pieces + 1, 2 * tile_px, LANES), jnp.float32),
            pltpu.VMEM((2, pieces + 1, tile_px, LANES), jnp.float32),
            pltpu.VMEM((2, blocks, tile_px, LANES), jnp.float32),
            pltpu.VMEM((2, pieces, tile_px, LANES), jnp.float32),
            pltpu.VMEM((2, pieces, tile_px, LANES), jnp.float32),
            pltpu.VMEM((2, groups, rows, tile_px), jnp.float32),
            pltpu.VMEM((2, groups, rows, tile_px), jnp.float32),
            pltpu.SemaphoreType.DMA((2,)),
            pltpu.SemaphoreType.DMA((2, blocks, groups)),
            pltpu.SemaphoreType.DMA((2, blocks, groups)),
            pltpu.SemaphoreType.DMA((2, blocks)),
        ],
        compiler_params=pltpu.CompilerParams(
            collective_id=0,
            has_side_effects=True,
            vmem_limit_bytes=24 * 1024 * 1024,
        ),
        name="exchange",
    )(materials, corners, gradient, field, *held)


def body(object_tiles, probe_wave, measured, positions, materials):
    own_object = object_tiles[0, :, 0]
    tile_px = own_object.shape[-1]
    length = probe_wave.shape[-1]
    row_step = TILE_COLS % lax.axis_size("tile")
    fold = row_step == 0
    gradient, field, held = patch_calls(
        own_object,
        probe_wave[0],
        measured[0, 0],
        positions[0].T,
        fold,
        functools.partial(shifted, axis="tile", steps=-1),
    )
    if not fold:
        from_above = shifted(gradient[:, :, tile_px:], "tile", row_step)
        gradient = gradient.at[:, :, :length].add(from_above)
    fitted = exchange_fit(gradient, field, held, positions[0].T, materials, fold)
    return fitted.reshape(1, 2, 1, tile_px, tile_px)


def solution(mesh):
    in_specs = (
        P("energy", None, "tile", None, None),
        P("energy", None, None, None),
        P("energy", "tile", None, None, None),
        P("tile", None, None),
        P(),
    )
    out_specs = P("energy", None, "tile", None, None)
    return jax.shard_map(body, mesh=mesh, in_specs=in_specs, out_specs=out_specs, check_vma=False)
```
